32 devices in a mesh: img: 2 (over x), sp: 2 (over core), tp: 8 (over z, y).
Axes of the slice: x: 2, y: 2, z: 4, core: 2. Of those that a mesh axis runs over, the one named last changes fastest.
Arguments:
- tokens: bfloat16 [16, 32, 6144], P(('img', 'tp'), 'sp'), parts along dimension 0, may hold values from -6 to 6
- up_weight: bfloat16 [6144, 24576], P('sp', 'tp'), may hold values from -0.078125 to 0.078125
- up_bias: float32 [24576], P('tp'), may hold values from -3 to 3
- conv_weight: float32 [3, 3, 24576], P(None, None, 'tp'), may hold values from -2 to 2
- conv_bias: float32 [24576], P('tp'), may hold values from -3 to 3
- down_weight: bfloat16 [24576, 6144], P('tp', 'sp'), may hold values from -0.0390625 to 0.0390625
- down_bias: float32 [6144], replicated, may hold values from -3 to 3
Outputs:
- projected: bfloat16 [16, 32, 6144], P(('img', 'tp'), 'sp'), parts along dimension 0
The draws below stay inside these ranges and needn't reach their ends.
There are 2 independent parts, one for each index of `img`. The reference program is written for one: setup_inputs(seed, part) draws one part's arguments, and reference() takes and returns one part's arrays. A program takes and returns all parts, laid end to end along the dimension named above; an argument that names none is the same for every part. Nothing has to cross between parts.
All inputs are finite; a program needn't handle non-finite values.
Results may differ from the reference program's by a relative error of at most 0.0053.
Values may be sent and summed in bfloat16 or wider, within the bound.
No kernel may reach another device: no remote copies, remote signals or barrier semaphores. Data moves between devices by JAX's collectives and lax.ppermute only.
A program may use at most 256 MiB of HBM per device.

```python
import jax
import jax.numpy as jnp

D = 6144
FF = 24576
GX = 8
GY = 32


def levels(key, dims, split, smallest, top_value):
    gain, own = 1.0, jax.random.fold_in(key, 6)
    for axis_at, parts in split:
        draws = jnp.exp(jax.random.uniform(jax.random.fold_in(own, axis_at), (parts,), jnp.float32, smallest / len(split), top_value / len(split)))
        gain = gain * jnp.repeat(draws, dims[axis_at] // parts).reshape([-1 if axis == axis_at else 1 for axis in range(len(dims))])
    return gain


def scatter_about(own_key, extent, deviation, bound, pieces=(), kind=jnp.bfloat16):
    array = deviation * jax.random.normal(own_key, extent, jnp.float32)
    if pieces:
        array = array * levels(own_key, extent, pieces, -0.22, 0.18)
    return jnp.clip(array, -bound, bound).astype(kind)


def setup_inputs(seed: int = 0, part: int = 0) -> dict:
    key_of = jax.random.split(jax.random.key(seed), 8)
    own_keys = jax.random.split(jax.random.fold_in(key_of[7], part), 8)
    return {
        "tokens": scatter_about(own_keys[0], (GX, GY, D), 1.0, 6.0, ((0, 8), (1, 2))),
        "up_weight": scatter_about(key_of[1], (D, FF), D ** -0.5, 0.078125, ((0, 2), (1, 8))),
        "up_bias": scatter_about(key_of[2], (FF,), 0.5, 3.0, ((0, 8),), jnp.float32),
        "conv_weight": scatter_about(key_of[3], (3, 3, FF), 9 ** -0.5, 2.0, ((2, 8),), jnp.float32),
        "conv_bias": scatter_about(key_of[4], (FF,), 0.5, 3.0, ((0, 8),), jnp.float32),
        "down_weight": scatter_about(key_of[5], (FF, D), FF ** -0.5, 0.0390625, ((0, 8), (1, 2))),
        "down_bias": scatter_about(key_of[6], (D,), 0.5, 3.0, (), jnp.float32),
    }


def depthwise_ref(hidden, conv_weight, conv_bias):
    padded = jnp.pad(hidden.astype(jnp.float32), ((1, 1), (1, 1), (0, 0)))
    extent_x = hidden.shape[0]
    extent_y = hidden.shape[1]
    summed = jnp.zeros(hidden.shape, jnp.float32) + conv_bias
    for offset_x in range(3):
        for offset_y in range(3):
            window = padded[offset_x:offset_x + extent_x, offset_y:offset_y + extent_y]
            summed = summed + window * conv_weight[offset_x, offset_y]
    return jax.nn.gelu(summed, approximate=False).astype(jnp.bfloat16)


def reference(tokens, up_weight, up_bias, conv_weight, conv_bias, down_weight, down_bias):
    extent_x = tokens.shape[0]
    extent_y = tokens.shape[1]
    width_model = tokens.shape[2]
    hidden_units = up_weight.shape[1]
    flat_tokens = tokens.reshape(extent_x * extent_y, width_model)
    hidden = jnp.dot(flat_tokens, up_weight, preferred_element_type=jnp.float32) + up_bias
    hidden = hidden.astype(jnp.bfloat16).reshape(extent_x, extent_y, hidden_units)
    mixed = depthwise_ref(hidden, conv_weight, conv_bias)
    output = jnp.dot(mixed.reshape(extent_x * extent_y, hidden_units), down_weight, preferred_element_type=jnp.float32) + down_bias
    return output.astype(jnp.bfloat16).reshape(extent_x, extent_y, width_model)
```

```python
import functools

import jax
import jax.numpy as jnp
from jax import lax
from jax.experimental import pallas as pl
from jax.experimental.pallas import tpu as pltpu
from jax.sharding import PartitionSpec as P

F32 = jnp.float32
BF16 = jnp.bfloat16
VMEM = pl.BlockSpec(memory_space=pltpu.VMEM)
HBM = pl.BlockSpec(memory_space=pltpu.HBM)
SMEM = pl.BlockSpec(memory_space=pltpu.SMEM)
MIB = 1 << 20

ERF_NUM = (0.00022905065861350646, 0.0034082910107109506, 0.050955695062380861, 0.18520832239976145, 1.128379143519084)
ERF_DEN = (
    -1.1791602954361697e-7,
    0.000023547966471313185,
    0.0010179625278914885,
    0.014070470171167667,
    0.11098505178285362,
    0.49746925110067538,
    1.0,
)


def tile_of(size, most):
    for tile in range(most, 0, -128):
        if size % tile == 0:
            return tile
    return size


def cost(flops, moved, transcendentals=0):
    return pl.CostEstimate(flops=int(flops), bytes_accessed=int(moved), transcendentals=int(transcendentals))


def params(limit):
    return pltpu.CompilerParams(vmem_limit_bytes=limit * MIB)


def row_copies(weight_ref, first, out_ref, sems):
    parts = sems.shape[0]
    step = out_ref.shape[0] // parts
    return [
        pltpu.make_async_copy(
            weight_ref.at[pl.ds(first + part * step, step)], out_ref.at[pl.ds(part * step, step)], sems.at[part]
        )
        for part in range(parts)
    ]


def fetch(info, weight, start, count, held, parts=4):
    own_bytes = count * weight.shape[1] * 2
    limit = max(1, (60 * MIB - held - own_bytes) // MIB - 8)

    def kernel(info_ref, weight_ref, out_ref, sems):
        copies = row_copies(weight_ref, pl.multiple_of(start(info_ref[0]), 16), out_ref, sems)
        for copy in copies:
            copy.start()
        for copy in copies:
            copy.wait()

    return pl.pallas_call(
        kernel,
        out_shape=pltpu.VMEM((count, weight.shape[1]), weight.dtype),
        in_specs=[SMEM, HBM],
        out_specs=VMEM,
        scratch_shapes=[pltpu.SemaphoreType.DMA((parts,))],
        cost_estimate=cost(0, 2 * count * weight.shape[1] * 2),
        compiler_params=params(limit),
    )(info, weight)


def up_other(info, slots, upper, lower, width):
    rows = slots[0].shape[0]
    depth = slots[0].shape[1]
    total = rows * len(slots)
    split = upper.shape[0]
    tile = tile_of(width, 768)
    high = tile_of(total, 256)

    def kernel(info_ref, *refs):
        slot_refs = refs[: len(slots)]
        upper_ref, lower_ref, out_ref, tokens_ref = refs[len(slots) :]
        for index, ref in enumerate(slot_refs):
            tokens_ref[index * rows : (index + 1) * rows, :] = ref[...]
        base = (1 - info_ref[0]) * width

        def body(step, carry):
            row, col = step // (width // tile), step % (width // tile)
            down = pl.ds(pl.multiple_of(row * high, high), high)
            across = pl.ds(pl.multiple_of(base + col * tile, 128), tile)
            product = jnp.dot(tokens_ref[down, :split], upper_ref[:, across], preferred_element_type=F32) + jnp.dot(
                tokens_ref[down, split:], lower_ref[:, across], preferred_element_type=F32
            )
            out_ref[down, pl.ds(pl.multiple_of(col * tile, 128), tile)] = product.astype(BF16)
            return carry

        lax.fori_loop(0, (total // high) * (width // tile), body, 0)

    return pl.pallas_call(
        kernel,
        out_shape=(
            pltpu.VMEM((total, width), BF16),
            pltpu.VMEM((total, depth), BF16),
        ),
        in_specs=[SMEM] + [VMEM] * (len(slots) + 2),
        out_specs=(VMEM, VMEM),
        cost_estimate=cost(2 * total * depth * width, 2 * depth * width),
        compiler_params=params(12),
    )(info, *slots, upper, lower)


def up_own(info, tokens, upper, lower, width):
    total, depth = tokens.shape
    split = upper.shape[0]
    tile = tile_of(width, 768)
    high = tile_of(total, 256)

    def kernel(info_ref, tokens_ref, upper_ref, lower_ref, out_ref):
        base = info_ref[0] * width

        def body(step, carry):
            row, col = step // (width // tile), step % (width // tile)
            down = pl.ds(pl.multiple_of(row * high, high), high)
            across = pl.ds(pl.multiple_of(base + col * tile, 128), tile)
            out_ref[down, pl.ds(pl.multiple_of(col * tile, 128), tile)] = jnp.dot(
                tokens_ref[down, :split], upper_ref[:, across], preferred_element_type=F32
            ) + jnp.dot(tokens_ref[down, split:], lower_ref[:, across], preferred_element_type=F32)
            return carry

        lax.fori_loop(0, (total // high) * (width // tile), body, 0)

    return pl.pallas_call(
        kernel,
        out_shape=pltpu.VMEM((total, width), F32),
        in_specs=[SMEM] + [VMEM] * 3,
        out_specs=VMEM,
        cost_estimate=cost(2 * total * depth * width, 2 * depth * width),
        compiler_params=params(12),
    )(info, tokens, upper, lower)


def gelu(value):
    arg = jnp.clip(value * 0.7071067811865476, -3.832506856900711, 3.832506856900711)
    square = arg * arg
    num = jnp.full_like(square, ERF_NUM[0])
    for coefficient in ERF_NUM[1:]:
        num = num * square + coefficient
    den = jnp.full_like(square, ERF_DEN[0])
    for coefficient in ERF_DEN[1:]:
        den = den * square + coefficient
    return 0.5 * value * (1.0 + arg * num / den)


def conv(info, own, received, up_bias, conv_weight, conv_bias, later, ring_size, lanes_of, grid_y):
    total, width = own.shape
    blocks = ring_size * lanes_of
    rows = total // blocks
    lanes = 128
    extent_x = total // grid_y

    def kernel(info_ref, own_ref, received_ref, up_bias_ref, weight_ref, bias_ref, later_ref, out_ref, later_out, hidden, sems):
        copies = row_copies(later_ref, pl.multiple_of(info_ref[0] * width, 16), later_out, sems)
        for copy in copies:
            copy.start()
        hidden[0:grid_y, :] = jnp.zeros((grid_y, lanes), F32)
        hidden[(extent_x + 1) * grid_y : (extent_x + 2) * grid_y, :] = jnp.zeros((grid_y, lanes), F32)
        at_y = lax.broadcasted_iota(jnp.int32, (grid_y, lanes), 0)
        first, last = at_y == 0, at_y == grid_y - 1
        base = info_ref[0] * width
        places = [
            lax.rem(info_ref[1] + (ring_size - j), ring_size) * lanes_of + lax.rem(info_ref[2] + q, lanes_of)
            for q in range(lanes_of)
            for j in range(ring_size)
        ]

        def body(col, carry):
            across = pl.ds(pl.multiple_of(col * lanes, lanes), lanes)
            absolute = pl.ds(pl.multiple_of(base + col * lanes, lanes), lanes)
            shift = up_bias_ref[:, absolute]
            for slot in range(blocks):
                down = slice(slot * rows, (slot + 1) * rows)
                value = own_ref[down, across] + received_ref[down, across].astype(F32) + shift
                target = pl.multiple_of(places[slot] * rows + grid_y, grid_y)
                hidden[pl.ds(target, rows), :] = value.astype(BF16).astype(F32)
            weights = [[weight_ref[a, b : b + 1, absolute] for b in range(3)] for a in range(3)]
            offset = bias_ref[:, absolute]
            for slot in range(blocks):
                for line in range(rows // grid_y):
                    start = places[slot] * rows + line * grid_y
                    near = [hidden[pl.ds(pl.multiple_of(start + a * grid_y, grid_y), grid_y), :] for a in range(3)]
                    sums = [near[0] * weights[0][b] + near[1] * weights[1][b] + near[2] * weights[2][b] for b in range(3)]
                    before = jnp.where(first, 0.0, pltpu.roll(sums[0], 1, axis=0))
                    after = jnp.where(last, 0.0, pltpu.roll(sums[2], grid_y - 1, axis=0))
                    value = sums[1] + before + after + offset
                    out_ref[slot * rows + line * grid_y : slot * rows + (line + 1) * grid_y, across] = gelu(value).astype(BF16)
            return carry

        lax.fori_loop(0, width // lanes, body, 0)
        for copy in copies:
            copy.wait()

    return pl.pallas_call(
        kernel,
        out_shape=(pltpu.VMEM((total, width), BF16), pltpu.VMEM((width, later.shape[1]), BF16)),
        in_specs=[SMEM] + [VMEM] * 5 + [HBM],
        out_specs=(VMEM, VMEM),
        scratch_shapes=[pltpu.VMEM(((extent_x + 2) * grid_y, lanes), F32), pltpu.SemaphoreType.DMA((4,))],
        cost_estimate=cost(60 * total * width, 8 * total * width),
        compiler_params=params(33),
    )(info, own, received, up_bias, conv_weight, conv_bias, later)


def down_own(info, mixed, weight, later):
    total, depth = mixed.shape
    width = weight.shape[1]
    tile = tile_of(width, 1024)
    high = tile_of(total, 256)

    def kernel(info_ref, mixed_ref, weight_ref, later_ref, out_ref, later_out, sems):
        copies = row_copies(later_ref, pl.multiple_of((1 - info_ref[0]) * depth, 16), later_out, sems)
        for copy in copies:
            copy.start()

        def body(step, carry):
            row, col = step // (width // tile), step % (width // tile)
            down = pl.ds(pl.multiple_of(row * high, high), high)
            across = pl.ds(pl.multiple_of(col * tile, tile), tile)
            out_ref[down, across] = jnp.dot(mixed_ref[down, :], weight_ref[:, across], preferred_element_type=F32)
            return carry

        lax.fori_loop(0, (total // high) * (width // tile), body, 0)
        for copy in copies:
            copy.wait()

    return pl.pallas_call(
        kernel,
        out_shape=(pltpu.VMEM((total, width), F32), pltpu.VMEM((depth, width), BF16)),
        in_specs=[SMEM] + [VMEM] * 2 + [HBM],
        out_specs=(VMEM, VMEM),
        scratch_shapes=[pltpu.SemaphoreType.DMA((4,))],
        cost_estimate=cost(2 * total * depth * width, 2 * depth * width),
        compiler_params=params(26),
    )(info, mixed, weight, later)


def down_other(mixed, weight, partial, kept):
    total, depth = mixed.shape
    width = weight.shape[1]
    tile = tile_of(width, 1024)

    def kernel(mixed_ref, weight_ref, partial_ref, keep_ref, *send_refs):
        def body(col, carry):
            across = pl.ds(pl.multiple_of(col * tile, tile), tile)
            for first in range(0, total, 256):
                high = min(256, total - first)
                value = partial_ref[first : first + high, across] + jnp.dot(
                    mixed_ref[first : first + high, :], weight_ref[:, across], preferred_element_type=F32
                )
                inside = max(0, min(high, kept - first))
                if inside:
                    keep_ref[first : first + inside, across] = value[:inside]
                if inside < high:
                    low = first + inside - kept
                    send_refs[0][low : low + high - inside, across] = value[inside:].astype(BF16)
            return carry

        lax.fori_loop(0, width // tile, body, 0)

    shapes = [pltpu.VMEM((kept, width), F32)]
    if kept < total:
        shapes.append(pltpu.VMEM((total - kept, width), BF16))
    return pl.pallas_call(
        kernel,
        out_shape=tuple(shapes),
        in_specs=[VMEM] * 3,
        out_specs=(VMEM,) * len(shapes),
        cost_estimate=cost(2 * total * depth * width, 2 * depth * width),
        compiler_params=params(12),
    )(mixed, weight, partial)


def tie(*values):
    return lax.optimization_barrier(values)


def local(tokens, up_weight, up_bias, conv_weight, conv_bias, down_weight, down_bias):
    cols, grid_half, width_model = tokens.shape
    half = width_model // 2
    units = up_weight.shape[1]
    units_half = units // 2
    grid_y = grid_half * 2
    rows = cols * grid_y

    count = lax.axis_size("tp")
    lanes = 2 if count % 2 == 0 else 1
    ring_size = count // lanes
    core = lax.axis_index("sp")
    mine = lax.axis_index("tp")
    ring_at, lane_at = mine // lanes, mine % lanes
    ring = [(t, (t + lanes) % count) for t in range(count)]
    cross = [(t, t ^ 1) for t in range(count)]
    swap = [(0, 1), (1, 0)]

    flat = tokens.reshape(cols * grid_half, width_model)
    keep = lax.dynamic_slice_in_dim(flat, core * half, half, axis=1)
    give = lax.dynamic_slice_in_dim(flat, (1 - core) * half, half, axis=1)
    take = lax.ppermute(give, "sp", swap)
    keep, take = (x.reshape(cols, 1, grid_half, half) for x in (keep, take))
    block = jnp.where(core == 0, jnp.concatenate([keep, take], 1), jnp.concatenate([take, keep], 1))
    block = block.reshape(rows, half)

    info = jnp.stack([core, ring_at, lane_at]).astype(jnp.int32)
    block, info = tie(block, info)

    up_split = half // 2
    up_bytes = up_split * units * 2
    fetches = [
        lambda: fetch(info, up_weight, lambda c: 0 * c, up_split, 0),
        lambda: fetch(info, up_weight, lambda c: 0 * c + up_split, up_split, up_bytes),
    ]

    column, beside, fetched = [block], [], []
    for step in range(ring_size):
        current = column[-1]
        pending = []
        if lanes > 1:
            pending.append(lax.ppermute(current, "tp", cross))
        if step < ring_size - 1:
            pending.append(lax.ppermute(current, "tp", ring))
        if fetches:
            fetched.append(fetches.pop(0)())
            pending.append(fetched[-1])
        done = list(tie(*pending))
        if lanes > 1:
            beside.append(done.pop(0))
        if step < ring_size - 1:
            column.append(done.pop(0))
        if done:
            fetched[-1] = done.pop(0)
    fetched += [make() for make in fetches]
    upper, lower = fetched
    slots = column + beside

    partial_other, gathered = up_other(info, slots, upper, lower, units_half)
    partial_received = lax.ppermute(partial_other, "sp", swap)
    partial_own = up_own(info, gathered, upper, lower, units_half)
    mixed, down_mine = conv(
        info,
        partial_own,
        partial_received,
        up_bias.reshape(1, units),
        conv_weight,
        conv_bias.reshape(1, units),
        down_weight,
        ring_size,
        lanes,
        grid_y,
    )
    mixed_received = lax.ppermute(mixed, "sp", swap)
    product, down_theirs = down_own(info, mixed, down_mine, down_weight)
    sums = down_other(mixed_received, down_theirs, product, ring_size * rows)
    kept = sums[0].reshape(ring_size, rows, half)

    order = list(range(1, ring_size)) + [0]
    if lanes > 1:
        sent = sums[1].reshape(ring_size, rows, half)
    travelling = None
    for position, j in enumerate(order):
        value = kept[j]
        if lanes > 1:
            value = value + lax.ppermute(sent[j], "tp", cross).astype(F32)
        if travelling is not None:
            value = value + travelling.astype(F32)
        if position < ring_size - 1:
            travelling = lax.ppermute(value.astype(BF16), "tp", ring)
    bias = lax.dynamic_slice_in_dim(down_bias, core * half, half)
    final = (value + bias).astype(BF16).reshape(cols, 2, grid_half, half)
    stay = lax.dynamic_index_in_dim(final, core, 1, keepdims=False)
    leave = lax.dynamic_index_in_dim(final, 1 - core, 1, keepdims=False)
    arrive = lax.ppermute(leave, "sp", swap)
    return jnp.where(core == 0, jnp.concatenate([stay, arrive], -1), jnp.concatenate([arrive, stay], -1))


def solution(mesh):
    placed = (
        P(("img", "tp"), "sp", None),
        P("sp", "tp"),
        P("tp"),
        P(None, None, "tp"),
        P("tp"),
        P("tp", "sp"),
        P(),
    )
    return jax.shard_map(
        local, mesh=mesh, in_specs=placed, out_specs=P(("img", "tp"), "sp", None), check_vma=False
    )
```

```python
import jax
import jax.numpy as jnp
from jax import lax
from jax.experimental import pallas as pl
from jax.experimental.pallas import tpu as pltpu
from jax.sharding import PartitionSpec as P

F32 = jnp.float32
BF16 = jnp.bfloat16
VMEM = pl.BlockSpec(memory_space=pltpu.VMEM)
HBM = pl.BlockSpec(memory_space=pltpu.HBM)
SMEM = pl.BlockSpec(memory_space=pltpu.SMEM)
MIB = 1 << 20

ERF_NUM = (0.00022905065861350646, 0.0034082910107109506, 0.050955695062380861, 0.18520832239976145, 1.128379143519084)
ERF_DEN = (
    -1.1791602954361697e-7,
    0.000023547966471313185,
    0.0010179625278914885,
    0.014070470171167667,
    0.11098505178285362,
    0.49746925110067538,
    1.0,
)


def tile_of(size, most):
    for tile in range(most, 0, -128):
        if size % tile == 0:
            return tile
    return size


def cost(flops, moved, transcendentals=0):
    return pl.CostEstimate(flops=int(flops), bytes_accessed=int(moved), transcendentals=int(transcendentals))


def params(limit):
    return pltpu.CompilerParams(vmem_limit_bytes=limit * MIB)


def row_copies(weight_ref, first, out_ref, sems):
    parts = sems.shape[0]
    step = out_ref.shape[0] // parts
    return [
        pltpu.make_async_copy(
            weight_ref.at[pl.ds(first + part * step, step)], out_ref.at[pl.ds(part * step, step)], sems.at[part]
        )
        for part in range(parts)
    ]


def fetch(info, weight, start, count, held, parts=4):
    own_bytes = count * weight.shape[1] * 2
    limit = max(1, (60 * MIB - held - own_bytes) // MIB - 8)

    def kernel(info_ref, weight_ref, out_ref, sems):
        copies = row_copies(weight_ref, pl.multiple_of(start(info_ref[0]), 16), out_ref, sems)
        for copy in copies:
            copy.start()
        for copy in copies:
            copy.wait()

    return pl.pallas_call(
        kernel,
        out_shape=pltpu.VMEM((count, weight.shape[1]), weight.dtype),
        in_specs=[SMEM, HBM],
        out_specs=VMEM,
        scratch_shapes=[pltpu.SemaphoreType.DMA((parts,))],
        cost_estimate=cost(0, 2 * count * weight.shape[1] * 2),
        compiler_params=params(limit),
    )(info, weight)


def gathered_rows(slot_refs, tokens_ref):
    rows = slot_refs[0].shape[0]
    for index, ref in enumerate(slot_refs):
        tokens_ref[index * rows : (index + 1) * rows, :] = ref[...]


def tiles(total, width, most, body):
    tile = tile_of(width, most)
    high = tile_of(total, 256)

    def step_body(step, carry):
        row, col = step // (width // tile), step % (width // tile)
        body(pl.ds(pl.multiple_of(row * high, high), high), pl.multiple_of(col * tile, tile), tile)
        return carry

    lax.fori_loop(0, (total // high) * (width // tile), step_body, 0)


def up_first(slots, weight):
    rows, depth = slots[0].shape
    total = rows * len(slots)
    width = weight.shape[1]

    def kernel(*refs):
        weight_ref, out_ref, tokens_ref = refs[len(slots) :]
        gathered_rows(refs[: len(slots)], tokens_ref)

        def body(down, col, tile):
            out_ref[down, pl.ds(col, tile)] = jnp.dot(
                tokens_ref[down, :], weight_ref[:, pl.ds(col, tile)], preferred_element_type=F32
            )

        tiles(total, width, 1024, body)

    return pl.pallas_call(
        kernel,
        out_shape=pltpu.VMEM((total, width), F32),
        in_specs=[VMEM] * (len(slots) + 1),
        out_specs=VMEM,
        scratch_shapes=[pltpu.VMEM((total, depth), BF16)],
        cost_estimate=cost(2 * total * depth * width, 2 * depth * width),
        compiler_params=params(12),
    )(*slots, weight)


def up_other(info, slots, weight, partial):
    rows, depth = slots[0].shape
    total = rows * len(slots)
    width = weight.shape[1] // 2

    def kernel(info_ref, *refs):
        weight_ref, partial_ref, out_ref, tokens_ref = refs[len(slots) :]
        gathered_rows(refs[: len(slots)], tokens_ref)
        base = (1 - info_ref[0]) * width

        def body(down, col, tile):
            across = pl.ds(pl.multiple_of(base + col, 128), tile)
            product = jnp.dot(tokens_ref[down, :], weight_ref[:, across], preferred_element_type=F32)
            out_ref[down, pl.ds(col, tile)] = (partial_ref[down, across] + product).astype(BF16)

        tiles(total, width, 768, body)

    return pl.pallas_call(
        kernel,
        out_shape=(pltpu.VMEM((total, width), BF16), pltpu.VMEM((total, depth), BF16)),
        in_specs=[SMEM] + [VMEM] * (len(slots) + 2),
        out_specs=(VMEM, VMEM),
        cost_estimate=cost(2 * total * depth * width, 2 * depth * width),
        compiler_params=params(12),
    )(info, *slots, weight, partial)


def up_own(info, tokens, weight, partial):
    total, depth = tokens.shape
    width = weight.shape[1] // 2

    def kernel(info_ref, tokens_ref, weight_ref, partial_ref, out_ref):
        base = info_ref[0] * width

        def body(down, col, tile):
            across = pl.ds(pl.multiple_of(base + col, 128), tile)
            product = jnp.dot(tokens_ref[down, :], weight_ref[:, across], preferred_element_type=F32)
            out_ref[down, pl.ds(col, tile)] = partial_ref[down, across] + product

        tiles(total, width, 768, body)

    return pl.pallas_call(
        kernel,
        out_shape=pltpu.VMEM((total, width), F32),
        in_specs=[SMEM] + [VMEM] * 3,
        out_specs=VMEM,
        cost_estimate=cost(2 * total * depth * width, 2 * depth * width),
        compiler_params=params(12),
    )(info, tokens, weight, partial)


def gelu(value):
    arg = jnp.clip(value * 0.7071067811865476, -3.832506856900711, 3.832506856900711)
    square = arg * arg
    num = jnp.full_like(square, ERF_NUM[0])
    for coefficient in ERF_NUM[1:]:
        num = num * square + coefficient
    den = jnp.full_like(square, ERF_DEN[0])
    for coefficient in ERF_DEN[1:]:
        den = den * square + coefficient
    return 0.5 * value * (1.0 + arg * num / den)


def conv(info, own, received, up_bias, conv_weight, conv_bias, later, ring_size, lanes_of, grid_y):
    total, width = own.shape
    blocks = ring_size * lanes_of
    rows = total // blocks
    lanes = 128
    extent_x = total // grid_y

    def kernel(info_ref, own_ref, received_ref, up_bias_ref, weight_ref, bias_ref, later_ref, out_ref, later_out, hidden, sems):
        copies = row_copies(later_ref, pl.multiple_of(info_ref[0] * width, 16), later_out, sems)
        for copy in copies:
            copy.start()
        hidden[0:grid_y, :] = jnp.zeros((grid_y, lanes), F32)
        hidden[(extent_x + 1) * grid_y : (extent_x + 2) * grid_y, :] = jnp.zeros((grid_y, lanes), F32)
        at_y = lax.broadcasted_iota(jnp.int32, (grid_y, lanes), 0)
        first, last = at_y == 0, at_y == grid_y - 1
        base = info_ref[0] * width
        places = [
            lax.rem(info_ref[1] + (ring_size - j), ring_size) * lanes_of + lax.rem(info_ref[2] + q, lanes_of)
            for q in range(lanes_of)
            for j in range(ring_size)
        ]

        def body(col, carry):
            across = pl.ds(pl.multiple_of(col * lanes, lanes), lanes)
            absolute = pl.ds(pl.multiple_of(base + col * lanes, lanes), lanes)
            shift = up_bias_ref[:, absolute]
            for slot in range(blocks):
                down = slice(slot * rows, (slot + 1) * rows)
                value = own_ref[down, across] + received_ref[down, across].astype(F32) + shift
                target = pl.multiple_of(places[slot] * rows + grid_y, grid_y)
                hidden[pl.ds(target, rows), :] = value.astype(BF16).astype(F32)
            weights = [[weight_ref[a, b : b + 1, absolute] for b in range(3)] for a in range(3)]
            offset = bias_ref[:, absolute]
            for slot in range(blocks):
                for line in range(rows // grid_y):
                    start = places[slot] * rows + line * grid_y
                    near = [hidden[pl.ds(pl.multiple_of(start + a * grid_y, grid_y), grid_y), :] for a in range(3)]
                    sums = [near[0] * weights[0][b] + near[1] * weights[1][b] + near[2] * weights[2][b] for b in range(3)]
                    before = jnp.where(first, 0.0, pltpu.roll(sums[0], 1, axis=0))
                    after = jnp.where(last, 0.0, pltpu.roll(sums[2], grid_y - 1, axis=0))
                    value = sums[1] + before + after + offset
                    out_ref[slot * rows + line * grid_y : slot * rows + (line + 1) * grid_y, across] = gelu(value).astype(BF16)
            return carry

        lax.fori_loop(0, width // lanes, body, 0)
        for copy in copies:
            copy.wait()

    return pl.pallas_call(
        kernel,
        out_shape=(pltpu.VMEM((total, width), BF16), pltpu.VMEM((width, later.shape[1]), BF16)),
        in_specs=[SMEM] + [VMEM] * 5 + [HBM],
        out_specs=(VMEM, VMEM),
        scratch_shapes=[pltpu.VMEM(((extent_x + 2) * grid_y, lanes), F32), pltpu.SemaphoreType.DMA((4,))],
        cost_estimate=cost(60 * total * width, 8 * total * width),
        compiler_params=params(33),
    )(info, own, received, up_bias, conv_weight, conv_bias, later)


def down_own(info, mixed, weight, later):
    total, depth = mixed.shape
    width = weight.shape[1]
    tile = tile_of(width, 1024)
    high = tile_of(total, 256)

    def kernel(info_ref, mixed_ref, weight_ref, later_ref, out_ref, later_out, sems):
        copies = row_copies(later_ref, pl.multiple_of((1 - info_ref[0]) * depth, 16), later_out, sems)
        for copy in copies:
            copy.start()

        def body(step, carry):
            row, col = step // (width // tile), step % (width // tile)
            down = pl.ds(pl.multiple_of(row * high, high), high)
            across = pl.ds(pl.multiple_of(col * tile, tile), tile)
            out_ref[down, across] = jnp.dot(mixed_ref[down, :], weight_ref[:, across], preferred_element_type=F32)
            return carry

        lax.fori_loop(0, (total // high) * (width // tile), body, 0)
        for copy in copies:
            copy.wait()

    return pl.pallas_call(
        kernel,
        out_shape=(pltpu.VMEM((total, width), F32), pltpu.VMEM((depth, width), BF16)),
        in_specs=[SMEM] + [VMEM] * 2 + [HBM],
        out_specs=(VMEM, VMEM),
        scratch_shapes=[pltpu.SemaphoreType.DMA((4,))],
        cost_estimate=cost(2 * total * depth * width, 2 * depth * width),
        compiler_params=params(26),
    )(info, mixed, weight, later)


def down_other(mixed, weight, partial, blocks, kept, start, width):
    total, depth = mixed.shape
    rows = total // blocks
    tile = tile_of(width, 768)

    def kernel(mixed_ref, weight_ref, partial_ref, *out_refs):
        def body(step, carry):
            col = pl.multiple_of(step * tile, tile)
            across = pl.ds(pl.multiple_of(start + col, 128), tile)
            here = pl.ds(col, tile)
            for first in range(0, total, 256):
                high = min(256, total - first)
                value = partial_ref[first : first + high, across] + jnp.dot(
                    mixed_ref[first : first + high, :], weight_ref[:, across], preferred_element_type=F32
                )
                for low in range(0, high, rows):
                    out_ref = out_refs[(first + low) // rows]
                    out_ref[:, here] = value[low : low + rows].astype(out_ref.dtype)
            return carry

        lax.fori_loop(0, width // tile, body, 0)

    return pl.pallas_call(
        kernel,
        out_shape=tuple(pltpu.VMEM((rows, width), F32 if block < kept else BF16) for block in range(blocks)),
        in_specs=[VMEM] * 3,
        out_specs=(VMEM,) * blocks,
        cost_estimate=cost(2 * total * depth * width, 2 * depth * width),
        compiler_params=params(12),
    )(mixed, weight, partial)


def finish(info, totals, bias, cols, grid_half):
    width = totals[0].shape[1]
    half = width * len(totals)

    def kernel(info_ref, *refs):
        bias_ref, stay_ref, leave_ref = refs[len(totals) :]
        core = info_ref[0]
        for index in range(len(totals)):
            shift = bias_ref[:, pl.ds(pl.multiple_of(core * half + index * width, 128), width)]
            for col in range(cols):
                for out_ref, side in ((stay_ref, core), (leave_ref, 1 - core)):
                    source = pl.ds(pl.multiple_of((2 * col + side) * grid_half, 8), grid_half)
                    out_ref[col, :, index * width : (index + 1) * width] = (refs[index][source, :] + shift).astype(BF16)

    return pl.pallas_call(
        kernel,
        out_shape=(pltpu.VMEM((cols, grid_half, half), BF16),) * 2,
        in_specs=[SMEM] + [VMEM] * (len(totals) + 1),
        out_specs=(VMEM, VMEM),
        cost_estimate=cost(4 * cols * grid_half * half, 8 * cols * grid_half * half),
        compiler_params=params(4),
    )(info, *totals, bias)


def tie(*values):
    return lax.optimization_barrier(values)


class Links:
    def __init__(self, count):
        self.lanes = 2 if count % 2 == 0 else 1
        self.ring = count // self.lanes
        self.upward = [(t, (t + self.lanes) % count) for t in range(count)]
        self.downward = [(t, s) for s, t in self.upward]
        self.pairs = [(t, t ^ 1) for t in range(count)]

    def up(self, value):
        return lax.ppermute(value, "tp", self.upward)

    def down(self, value):
        return lax.ppermute(value, "tp", self.downward)

    def cross(self, value):
        return lax.ppermute(value, "tp", self.pairs)


def gather_steps(links, block, tree, extras):
    ring = links.ring
    tree = tree and links.lanes > 1 and ring > 2
    column, beside = {0: block}, {}
    for step in range(1, ring + 1):
        moves = []
        if step < ring:
            moves.append((column, step, links.up(column[step - 1])))
        if links.lanes > 1 and not (tree and step == ring):
            moves.append((beside, step - 1, links.cross(column[step - 1])))
        if tree and step == 2:
            moves.append((beside, ring - 1, links.down(beside[0])))
        made = extras.get(step)
        yield
        values = [value for _, _, value in moves]
        if made is not None:
            values.append(made())
        if not values:
            continue
        done = tie(*values)
        for (where, slot, _), value in zip(moves, done):
            where[slot] = value
        if made is not None:
            extras[step] = done[-1]
    yield [column[j] for j in range(ring)] + [beside[j] for j in range(ring) if links.lanes > 1]


def scatter_steps(links, kept, sent, tree):
    ring = links.ring
    sent = list(sent)
    if tree and links.lanes > 1 and ring > 2:
        total = kept[ring - 1]
        for slot in range(ring - 2, -1, -1):
            moves = [links.down(total.astype(BF16)), links.cross(sent[slot])]
            if slot == 1:
                moves.append(links.up(sent[ring - 1]))
            yield
            count = len(moves)
            arrived = tie(*moves, *sent)
            moves, sent = arrived[:count], list(arrived[count:])
            total = kept[slot] + moves[0].astype(F32) + moves[1].astype(F32)
            if slot == 1:
                sent[0] = (sent[0].astype(F32) + moves[2].astype(F32)).astype(BF16)
    else:
        total = None
        for slot in list(range(1, ring)) + [0]:
            moves = [links.cross(sent[slot])] if links.lanes > 1 else []
            if total is not None:
                moves.append(links.up(total.astype(BF16)))
            yield
            count = len(moves)
            arrived = tie(*moves, *sent) if moves else tuple(sent)
            moves, sent = arrived[:count], list(arrived[count:])
            total = kept[slot]
            for value in moves:
                total = total + value.astype(F32)
    yield total


def interleave(streams):
    results = [None] * len(streams)
    live = list(range(len(streams)))
    while live:
        for index in list(live):
            try:
                results[index] = next(streams[index])
            except StopIteration:
                live.remove(index)
    return results


def local(tokens, up_weight, up_bias, conv_weight, conv_bias, down_weight, down_bias):
    cols, grid_half, width_model = tokens.shape
    half = width_model // 2
    part = half // 2
    units = up_weight.shape[1]
    units_half = units // 2
    grid_y = grid_half * 2
    rows = cols * grid_y

    links = Links(lax.axis_size("tp"))
    core = lax.axis_index("sp")
    mine = lax.axis_index("tp")
    swap = [(0, 1), (1, 0)]
    info = jnp.stack([core, mine // links.lanes, mine % links.lanes]).astype(jnp.int32)

    flat = tokens.reshape(cols * grid_half, width_model)
    keep = lax.dynamic_slice_in_dim(flat, core * half, half, axis=1)
    give = lax.dynamic_slice_in_dim(flat, (1 - core) * half, half, axis=1)
    take = lax.ppermute(give, "sp", swap)
    keep, take = (x.reshape(cols, 1, grid_half, half) for x in (keep, take))
    block = jnp.where(core == 0, jnp.concatenate([keep, take], 1), jnp.concatenate([take, keep], 1))
    block = block.reshape(rows, half)
    block_a, block_b, info = tie(block[:, :part], block[:, part:], info)

    part_bytes = part * units * 2
    extras_a = {}
    extras_b = {
        1: lambda: fetch(info, up_weight, lambda c: 0 * c, part, 0),
        2: lambda: fetch(info, up_weight, lambda c: 0 * c + part, part, part_bytes),
    }
    slots_a, slots_b = interleave(
        [gather_steps(links, block_a, False, extras_a), gather_steps(links, block_b, True, extras_b)]
    )
    upper, lower = (made if not callable(made) else made() for made in (extras_b[1], extras_b[2]))

    first = up_first(slots_a, upper)
    partial_other, tokens_b = up_other(info, slots_b, lower, first)
    partial_received = lax.ppermute(partial_other, "sp", swap)
    partial_own = up_own(info, tokens_b, lower, first)
    mixed, down_mine = conv(
        info,
        partial_own,
        partial_received,
        up_bias.reshape(1, units),
        conv_weight,
        conv_bias.reshape(1, units),
        down_weight,
        links.ring,
        links.lanes,
        grid_y,
    )
    mixed_received = lax.ppermute(mixed, "sp", swap)
    product, down_theirs = down_own(info, mixed, down_mine, down_weight)

    streams = []
    for start, tree in ((0, False), (part, True)):
        sums = down_other(mixed_received, down_theirs, product, len(slots_a), links.ring, start, part)
        streams.append(scatter_steps(links, sums[: links.ring], sums[links.ring :], tree))
    totals = interleave(streams)

    stay, leave = finish(info, totals, down_bias.reshape(1, width_model), cols, grid_half)
    arrive = lax.ppermute(leave, "sp", swap)
    return jnp.where(core == 0, jnp.concatenate([stay, arrive], -1), jnp.concatenate([arrive, stay], -1))


def solution(mesh):
    placed = (
        P(("img", "tp"), "sp", None),
        P("sp", "tp"),
        P("tp"),
        P(None, None, "tp"),
        P("tp"),
        P("tp", "sp"),
        P(),
    )
    return jax.shard_map(
        local, mesh=mesh, in_specs=placed, out_specs=P(("img", "tp"), "sp", None), check_vma=False
    )
```

```python
import jax
import jax.numpy as jnp
from jax import lax
from jax.experimental import pallas as pl
from jax.experimental.pallas import tpu as pltpu
from jax.sharding import PartitionSpec as P

F32 = jnp.float32
BF16 = jnp.bfloat16
VMEM = pl.BlockSpec(memory_space=pltpu.VMEM)
HBM = pl.BlockSpec(memory_space=pltpu.HBM)
SMEM = pl.BlockSpec(memory_space=pltpu.SMEM)
MIB = 1 << 20

ERF_NUM = (0.00022905065861350646, 0.0034082910107109506, 0.050955695062380861, 0.18520832239976145, 1.128379143519084)
ERF_DEN = (
    -1.1791602954361697e-7,
    0.000023547966471313185,
    0.0010179625278914885,
    0.014070470171167667,
    0.11098505178285362,
    0.49746925110067538,
    1.0,
)


def tile_of(size, most):
    for tile in range(most, 0, -128):
        if size % tile == 0:
            return tile
    return size


def cost(flops, moved, transcendentals=0):
    return pl.CostEstimate(flops=int(flops), bytes_accessed=int(moved), transcendentals=int(transcendentals))


def params(limit):
    return pltpu.CompilerParams(vmem_limit_bytes=limit * MIB)


def row_copies(weight_ref, first, out_ref, sems):
    parts = sems.shape[0]
    step = out_ref.shape[0] // parts
    return [
        pltpu.make_async_copy(
            weight_ref.at[pl.ds(first + part * step, step)], out_ref.at[pl.ds(part * step, step)], sems.at[part]
        )
        for part in range(parts)
    ]


def fetch(info, weight, start, count, held, parts=4):
    own_bytes = count * weight.shape[1] * 2
    limit = max(1, (60 * MIB - held - own_bytes) // MIB - 8)

    def kernel(info_ref, weight_ref, out_ref, sems):
        copies = row_copies(weight_ref, pl.multiple_of(start(info_ref[0]), 16), out_ref, sems)
        for copy in copies:
            copy.start()
        for copy in copies:
            copy.wait()

    return pl.pallas_call(
        kernel,
        out_shape=pltpu.VMEM((count, weight.shape[1]), weight.dtype),
        in_specs=[SMEM, HBM],
        out_specs=VMEM,
        scratch_shapes=[pltpu.SemaphoreType.DMA((parts,))],
        cost_estimate=cost(0, 2 * count * weight.shape[1] * 2),
        compiler_params=params(limit),
    )(info, weight)


def gathered_rows(slot_refs, tokens_ref):
    rows = slot_refs[0].shape[0]
    for index, ref in enumerate(slot_refs):
        tokens_ref[index * rows : (index + 1) * rows, :] = ref[...]


def tiles(total, width, most, body):
    tile = tile_of(width, most)
    high = tile_of(total, 256)

    def step_body(step, carry):
        row, col = step // (width // tile), step % (width // tile)
        body(pl.ds(pl.multiple_of(row * high, high), high), pl.multiple_of(col * tile, tile), tile)
        return carry

    lax.fori_loop(0, (total // high) * (width // tile), step_body, 0)


def up_near(info, slots, upper, lower):
    rows, depth = slots[0].shape
    total = rows * len(slots)
    split = upper.shape[0]
    width = upper.shape[1] // 2

    def kernel(info_ref, *refs):
        upper_ref, lower_ref, other_ref, own_ref, tokens_ref = refs[len(slots) :]
        gathered_rows(refs[: len(slots)], tokens_ref)
        for side, out_ref in ((1 - info_ref[0], other_ref), (info_ref[0], own_ref)):
            product_tiles(tokens_ref, upper_ref, lower_ref, side * width, out_ref)

    return pl.pallas_call(
        kernel,
        out_shape=(pltpu.VMEM((total, width), BF16), pltpu.VMEM((total, width), F32)),
        in_specs=[SMEM] + [VMEM] * (len(slots) + 2),
        out_specs=(VMEM, VMEM),
        scratch_shapes=[pltpu.VMEM((total, depth), BF16)],
        cost_estimate=cost(4 * total * depth * width, 2 * depth * width),
        compiler_params=params(10),
    )(info, *slots, upper, lower)


def product_tiles(tokens_ref, upper_ref, lower_ref, base, out_ref):
    split = upper_ref.shape[0]

    def body(down, col, tile):
        across = pl.ds(pl.multiple_of(base + col, 128), tile)
        product = jnp.dot(tokens_ref[down, :split], upper_ref[:, across], preferred_element_type=F32) + jnp.dot(
            tokens_ref[down, split:], lower_ref[:, across], preferred_element_type=F32
        )
        out_ref[down, pl.ds(col, tile)] = product.astype(out_ref.dtype)

    tiles(*out_ref.shape, 768, body)


def up_other(info, slots, upper, lower):
    rows, depth = slots[0].shape
    total = rows * len(slots)
    width = upper.shape[1] // 2

    def kernel(info_ref, *refs):
        upper_ref, lower_ref, out_ref, tokens_ref = refs[len(slots) :]
        gathered_rows(refs[: len(slots)], tokens_ref)
        product_tiles(tokens_ref, upper_ref, lower_ref, (1 - info_ref[0]) * width, out_ref)

    return pl.pallas_call(
        kernel,
        out_shape=(pltpu.VMEM((total, width), BF16), pltpu.VMEM((total, depth), BF16)),
        in_specs=[SMEM] + [VMEM] * (len(slots) + 2),
        out_specs=(VMEM, VMEM),
        cost_estimate=cost(2 * total * depth * width, 2 * depth * width),
        compiler_params=params(10),
    )(info, *slots, upper, lower)


def up_own(info, tokens, upper, lower):
    total, depth = tokens.shape
    width = upper.shape[1] // 2

    def kernel(info_ref, tokens_ref, upper_ref, lower_ref, out_ref):
        product_tiles(tokens_ref, upper_ref, lower_ref, info_ref[0] * width, out_ref)

    return pl.pallas_call(
        kernel,
        out_shape=pltpu.VMEM((total, width), F32),
        in_specs=[SMEM] + [VMEM] * 3,
        out_specs=VMEM,
        cost_estimate=cost(2 * total * depth * width, 2 * depth * width),
        compiler_params=params(10),
    )(info, tokens, upper, lower)


def gelu(value):
    arg = jnp.clip(value * 0.7071067811865476, -3.832506856900711, 3.832506856900711)
    square = arg * arg
    num = jnp.full_like(square, ERF_NUM[0])
    for coefficient in ERF_NUM[1:]:
        num = num * square + coefficient
    den = jnp.full_like(square, ERF_DEN[0])
    for coefficient in ERF_DEN[1:]:
        den = den * square + coefficient
    return 0.5 * value * (1.0 + arg * num / den)


def conv(info, own, received, up_bias, conv_weight, conv_bias, later, ring_size, lanes_of, grid_y):
    width = own[0].shape[1]
    rows = own[0].shape[0] // ring_size
    blocks = ring_size * lanes_of
    total = rows * blocks
    lanes = 128
    extent_x = total // grid_y

    def kernel(info_ref, *refs):
        own_refs, received_refs = refs[:lanes_of], refs[lanes_of : 2 * lanes_of]
        up_bias_ref, weight_ref, bias_ref, later_ref, out_ref, later_out, hidden, sems = refs[2 * lanes_of :]
        copies = row_copies(later_ref, pl.multiple_of(info_ref[0] * width, 16), later_out, sems)
        for copy in copies:
            copy.start()
        hidden[0:grid_y, :] = jnp.zeros((grid_y, lanes), F32)
        hidden[(extent_x + 1) * grid_y : (extent_x + 2) * grid_y, :] = jnp.zeros((grid_y, lanes), F32)
        at_y = lax.broadcasted_iota(jnp.int32, (grid_y, lanes), 0)
        first, last = at_y == 0, at_y == grid_y - 1
        base = info_ref[0] * width
        places = [
            lax.rem(info_ref[1] + (ring_size - j), ring_size) * lanes_of + lax.rem(info_ref[2] + q, lanes_of)
            for q in range(lanes_of)
            for j in range(ring_size)
        ]

        def body(col, carry):
            across = pl.ds(pl.multiple_of(col * lanes, lanes), lanes)
            absolute = pl.ds(pl.multiple_of(base + col * lanes, lanes), lanes)
            shift = up_bias_ref[:, absolute]
            for slot in range(blocks):
                q, j = slot // ring_size, slot % ring_size
                down = slice(j * rows, (j + 1) * rows)
                value = own_refs[q][down, across] + received_refs[q][down, across].astype(F32) + shift
                target = pl.multiple_of(places[slot] * rows + grid_y, grid_y)
                hidden[pl.ds(target, rows), :] = value.astype(BF16).astype(F32)
            weights = [[weight_ref[a, b : b + 1, absolute] for b in range(3)] for a in range(3)]
            offset = bias_ref[:, absolute]
            for slot in range(blocks):
                for line in range(rows // grid_y):
                    start = places[slot] * rows + line * grid_y
                    near = [hidden[pl.ds(pl.multiple_of(start + a * grid_y, grid_y), grid_y), :] for a in range(3)]
                    sums = [near[0] * weights[0][b] + near[1] * weights[1][b] + near[2] * weights[2][b] for b in range(3)]
                    before = jnp.where(first, 0.0, pltpu.roll(sums[0], 1, axis=0))
                    after = jnp.where(last, 0.0, pltpu.roll(sums[2], grid_y - 1, axis=0))
                    value = sums[1] + before + after + offset
                    out_ref[slot * rows + line * grid_y : slot * rows + (line + 1) * grid_y, across] = gelu(value).astype(BF16)
            return carry

        lax.fori_loop(0, width // lanes, body, 0)
        for copy in copies:
            copy.wait()

    return pl.pallas_call(
        kernel,
        out_shape=(pltpu.VMEM((total, width), BF16), pltpu.VMEM((width, later.shape[1]), BF16)),
        in_specs=[SMEM] + [VMEM] * (2 * lanes_of + 3) + [HBM],
        out_specs=(VMEM, VMEM),
        scratch_shapes=[pltpu.VMEM(((extent_x + 2) * grid_y, lanes), F32), pltpu.SemaphoreType.DMA((4,))],
        cost_estimate=cost(60 * total * width, 8 * total * width),
        compiler_params=params(33),
    )(info, *own, *received, up_bias, conv_weight, conv_bias, later)


def down_own(info, mixed, weight, later):
    total, depth = mixed.shape
    width = weight.shape[1]
    tile = tile_of(width, 1024)
    high = tile_of(total, 256)

    def kernel(info_ref, mixed_ref, weight_ref, later_ref, out_ref, later_out, sems):
        copies = row_copies(later_ref, pl.multiple_of((1 - info_ref[0]) * depth, 16), later_out, sems)
        for copy in copies:
            copy.start()

        def body(step, carry):
            row, col = step // (width // tile), step % (width // tile)
            down = pl.ds(pl.multiple_of(row * high, high), high)
            across = pl.ds(pl.multiple_of(col * tile, tile), tile)
            out_ref[down, across] = jnp.dot(mixed_ref[down, :], weight_ref[:, across], preferred_element_type=F32)
            return carry

        lax.fori_loop(0, (total // high) * (width // tile), body, 0)
        for copy in copies:
            copy.wait()

    return pl.pallas_call(
        kernel,
        out_shape=(pltpu.VMEM((total, width), F32), pltpu.VMEM((depth, width), BF16)),
        in_specs=[SMEM] + [VMEM] * 2 + [HBM],
        out_specs=(VMEM, VMEM),
        scratch_shapes=[pltpu.SemaphoreType.DMA((4,))],
        cost_estimate=cost(2 * total * depth * width, 2 * depth * width),
        compiler_params=params(26),
    )(info, mixed, weight, later)


def down_other(mixed, weight, partial, rows, first, blocks, kind):
    depth = mixed.shape[1]
    width = weight.shape[1]
    total = rows * blocks
    tile = tile_of(width, 1024)
    high = rows * max(n for n in range(1, blocks + 1) if blocks % n == 0 and rows * n <= max(256, rows))

    def kernel(mixed_ref, weight_ref, partial_ref, *out_refs):
        def body(step, carry):
            across = pl.ds(pl.multiple_of(step * tile, tile), tile)
            for start in range(0, total, high):
                down = slice(first + start, first + start + high)
                value = partial_ref[down, across] + jnp.dot(
                    mixed_ref[down, :], weight_ref[:, across], preferred_element_type=F32
                )
                for low in range(0, high, rows):
                    out_refs[(start + low) // rows][:, across] = value[low : low + rows].astype(kind)
            return carry

        lax.fori_loop(0, width // tile, body, 0)

    return pl.pallas_call(
        kernel,
        out_shape=(pltpu.VMEM((rows, width), kind),) * blocks,
        in_specs=[VMEM] * 3,
        out_specs=(VMEM,) * blocks,
        cost_estimate=cost(2 * total * depth * width, 2 * depth * width),
        compiler_params=params(10),
    )(mixed, weight, partial)


def finish(info, totals, bias, cols, grid_half):
    width = totals[0].shape[1]
    half = width * len(totals)

    def kernel(info_ref, *refs):
        bias_ref, stay_ref, leave_ref = refs[len(totals) :]
        core = info_ref[0]
        for index in range(len(totals)):
            shift = bias_ref[:, pl.ds(pl.multiple_of(core * half + index * width, 128), width)]
            for col in range(cols):
                for out_ref, side in ((stay_ref, core), (leave_ref, 1 - core)):
                    source = pl.ds(pl.multiple_of((2 * col + side) * grid_half, 8), grid_half)
                    out_ref[col, :, index * width : (index + 1) * width] = (refs[index][source, :] + shift).astype(BF16)

    return pl.pallas_call(
        kernel,
        out_shape=(pltpu.VMEM((cols, grid_half, half), BF16),) * 2,
        in_specs=[SMEM] + [VMEM] * (len(totals) + 1),
        out_specs=(VMEM, VMEM),
        cost_estimate=cost(4 * cols * grid_half * half, 8 * cols * grid_half * half),
        compiler_params=params(4),
    )(info, *totals, bias)


def tie(*values):
    return lax.optimization_barrier(values)


class Links:
    def __init__(self, count):
        self.lanes = 2 if count % 2 == 0 else 1
        self.ring = count // self.lanes
        self.upward = [(t, (t + self.lanes) % count) for t in range(count)]
        self.downward = [(t, s) for s, t in self.upward]
        self.pairs = [(t, t ^ 1) for t in range(count)]

    def up(self, value):
        return lax.ppermute(value, "tp", self.upward)

    def down(self, value):
        return lax.ppermute(value, "tp", self.downward)

    def cross(self, value):
        return lax.ppermute(value, "tp", self.pairs)


def gather(links, block, fetches):
    ring = links.ring
    half_way = ring // 2
    column, beside = {0: block}, {}
    first, second = fetches

    def hand(slot):
        if links.lanes > 1:
            beside[slot] = links.cross(column[slot])

    if ring > 1:
        column[1] = links.up(block)
    hand(0)
    upper = first()
    if ring > 2:
        if links.lanes > 1:
            late, upper, beside[0] = tie(block, upper, beside[0])
        else:
            late, upper = tie(block, upper)
        column[ring - 1] = links.down(late)
    if ring > 1:
        hand(1)
    if half_way > 1:
        column[2] = links.up(column[1])
    lower = second(column[1] if ring > 1 else block)
    for distance in range(1, half_way + 1):
        if distance > 2:
            column[distance] = links.up(column[distance - 1])
        if distance > 1:
            hand(distance)
        if 1 < distance < ring - half_way:
            column[ring - distance] = links.down(column[ring - distance + 1])
        if distance < ring - half_way:
            hand(ring - distance)
    return [column[j] for j in range(ring)], [beside[j] for j in range(ring) if links.lanes > 1], upper, lower


def scatter(links, far, make_near):
    ring = links.ring
    half_way = ring // 2
    upper_chain = list(range(half_way, 0, -1))
    lower_chain = list(range(half_way + 1, ring))
    order = [slot for pair in zip(upper_chain, lower_chain) for slot in pair]
    order += [slot for slot in upper_chain + lower_chain if slot not in order] + [0]
    far = list(far)
    crossed, arrived, ready = {}, {slot: [] for slot in range(ring)}, {}
    if links.lanes > 1:
        crossed[order[0]] = links.cross(far[order[0]])
    near = make_near()
    for position, slot in enumerate(order):
        if links.lanes > 1 and position + 1 < ring:
            after = order[position + 1]
            token = near[0] if position == 0 else ready[order[position - 1]]
            far[after], token = tie(far[after], token)
            if position == 0:
                near[0] = token
            else:
                ready[order[position - 1]] = token
            crossed[after] = links.cross(far[after])
        terms = arrived[slot] + ([crossed[slot]] if links.lanes > 1 else [])
        total = near[slot]
        for term in terms:
            total = total + term.astype(F32)
        if slot == 0:
            return total
        ready[slot] = total.astype(BF16)
        if slot <= half_way:
            arrived[slot - 1].append(links.down(ready[slot]))
        else:
            arrived[(slot + 1) % ring].append(links.up(ready[slot]))


def local(tokens, up_weight, up_bias, conv_weight, conv_bias, down_weight, down_bias):
    cols, grid_half, width_model = tokens.shape
    half = width_model // 2
    part = half // 2
    units = up_weight.shape[1]
    units_half = units // 2
    grid_y = grid_half * 2
    rows = cols * grid_y

    links = Links(lax.axis_size("tp"))
    core = lax.axis_index("sp")
    mine = lax.axis_index("tp")
    swap = [(0, 1), (1, 0)]
    info = jnp.stack([core, mine // links.lanes, mine % links.lanes]).astype(jnp.int32)

    flat = tokens.reshape(cols * grid_half, width_model)
    keep = lax.dynamic_slice_in_dim(flat, core * half, half, axis=1)
    give = lax.dynamic_slice_in_dim(flat, (1 - core) * half, half, axis=1)
    take = lax.ppermute(give, "sp", swap)
    keep, take = (x.reshape(cols, 1, grid_half, half) for x in (keep, take))
    block = jnp.where(core == 0, jnp.concatenate([keep, take], 1), jnp.concatenate([take, keep], 1))
    block = block.reshape(rows, half)
    block, info = tie(block, info)

    part_bytes = part * units * 2

    def fetch_lower(token):
        late, _ = tie(info, token)
        return fetch(late, up_weight, lambda c: 0 * c + part, part, part_bytes)

    near, far, upper, lower = gather(
        links, block, (lambda: fetch(info, up_weight, lambda c: 0 * c, part, 0), fetch_lower)
    )

    near_other, near_own = up_near(info, near, upper, lower)
    own, received = [near_own], [lax.ppermute(near_other, "sp", swap)]
    if far:
        far_other, tokens_far = up_other(info, far, upper, lower)
        received.append(lax.ppermute(far_other, "sp", swap))
        own.append(up_own(info, tokens_far, upper, lower))
    mixed, down_mine = conv(
        info,
        own,
        received,
        up_bias.reshape(1, units),
        conv_weight,
        conv_bias.reshape(1, units),
        down_weight,
        links.ring,
        links.lanes,
        grid_y,
    )
    mixed_received = lax.ppermute(mixed, "sp", swap)
    product, down_theirs = down_own(info, mixed, down_mine, down_weight)

    sent = []
    if far:
        sent = down_other(mixed_received, down_theirs, product, rows, links.ring * rows, links.ring, BF16)
    total = scatter(
        links, sent, lambda: list(down_other(mixed_received, down_theirs, product, rows, 0, links.ring, F32))
    )
    totals = [total]

    stay, leave = finish(info, totals, down_bias.reshape(1, width_model), cols, grid_half)
    arrive = lax.ppermute(leave, "sp", swap)
    return jnp.where(core == 0, jnp.concatenate([stay, arrive], -1), jnp.concatenate([arrive, stay], -1))


def solution(mesh):
    placed = (
        P(("img", "tp"), "sp", None),
        P("sp", "tp"),
        P("tp"),
        P(None, None, "tp"),
        P("tp"),
        P("tp", "sp"),
        P(),
    )
    return jax.shard_map(
        local, mesh=mesh, in_specs=placed, out_specs=P(("img", "tp"), "sp", None), check_vma=False
    )
```

```python
import jax
import jax.numpy as jnp
from jax import lax
from jax.experimental import pallas as pl
from jax.experimental.pallas import tpu as pltpu
from jax.sharding import PartitionSpec as P

F32 = jnp.float32
BF16 = jnp.bfloat16
VMEM = pl.BlockSpec(memory_space=pltpu.VMEM)
HBM = pl.BlockSpec(memory_space=pltpu.HBM)
SMEM = pl.BlockSpec(memory_space=pltpu.SMEM)
MIB = 1 << 20


def tile_of(size, most):
    for tile in range(most, 0, -128):
        if size % tile == 0:
            return tile
    return size


def cost(flops, moved, transcendentals=0):
    return pl.CostEstimate(flops=int(flops), bytes_accessed=int(moved), transcendentals=int(transcendentals))


def params(limit):
    return pltpu.CompilerParams(vmem_limit_bytes=limit * MIB)


def row_copies(weight_ref, first, out_ref, sems):
    parts = sems.shape[0]
    step = out_ref.shape[0] // parts
    return [
        pltpu.make_async_copy(
            weight_ref.at[pl.ds(first + part * step, step)], out_ref.at[pl.ds(part * step, step)], sems.at[part]
        )
        for part in range(parts)
    ]


def fetch(info, weight, start, count, held, parts=4):
    own_bytes = count * weight.shape[1] * 2
    limit = max(1, (60 * MIB - held - own_bytes) // MIB - 8)

    def kernel(info_ref, weight_ref, out_ref, sems):
        copies = row_copies(weight_ref, pl.multiple_of(start(info_ref[0]), 16), out_ref, sems)
        for copy in copies:
            copy.start()
        for copy in copies:
            copy.wait()

    return pl.pallas_call(
        kernel,
        out_shape=pltpu.VMEM((count, weight.shape[1]), weight.dtype),
        in_specs=[SMEM, HBM],
        out_specs=VMEM,
        scratch_shapes=[pltpu.SemaphoreType.DMA((parts,))],
        cost_estimate=cost(0, 2 * count * weight.shape[1] * 2),
        compiler_params=params(limit),
    )(info, weight)


def gathered_rows(slot_refs, tokens_ref):
    start = 0
    for ref in slot_refs:
        tokens_ref[start : start + ref.shape[0], :] = ref[...]
        start += ref.shape[0]


def tiles(total, width, most, body):
    tile = tile_of(width, most)
    high = tile_of(total, 256) if total > 256 else total

    def step_body(step, carry):
        row, col = step // (width // tile), step % (width // tile)
        body(pl.ds(pl.multiple_of(row * high, high), high), pl.multiple_of(col * tile, tile), tile)
        return carry

    lax.fori_loop(0, (total // high) * (width // tile), step_body, 0)


def up_early(info, slots, upper, weight):
    depth = slots[0].shape[1]
    total = sum(slot.shape[0] for slot in slots)
    split, units = upper.shape
    width = units // 2
    parts = 2
    step = (depth - split) // parts

    def kernel(info_ref, *refs):
        upper_ref, weight_ref, other_ref, own_ref, lower_ref, tokens_ref, sums_ref, sems = refs[len(slots) :]
        copies = row_copies(weight_ref, split, lower_ref, sems)
        for copy in copies:
            copy.start()
        gathered_rows(refs[: len(slots)], tokens_ref)

        def first(down, col, tile):
            across = pl.ds(col, tile)
            sums_ref[down, across] = jnp.dot(tokens_ref[down, :split], upper_ref[:, across], preferred_element_type=F32)

        tiles(total, units, 768, first)
        for part, copy in enumerate(copies):
            copy.wait()
            deep = slice(part * step, (part + 1) * step)
            features = slice(split + part * step, split + (part + 1) * step)

            def more(down, col, tile):
                across = pl.ds(col, tile)
                sums_ref[down, across] += jnp.dot(
                    tokens_ref[down, features], lower_ref[deep, across], preferred_element_type=F32
                )

            def last(out_ref, base):
                def body(down, col, tile):
                    across = pl.ds(pl.multiple_of(base + col, 128), tile)
                    value = sums_ref[down, across] + jnp.dot(
                        tokens_ref[down, features], lower_ref[deep, across], preferred_element_type=F32
                    )
                    out_ref[down, pl.ds(col, tile)] = value.astype(out_ref.dtype)

                return body

            if part < parts - 1:
                tiles(total, units, 768, more)
            else:
                tiles(total, width, 768, last(other_ref, (1 - info_ref[0]) * width))
                tiles(total, width, 768, last(own_ref, info_ref[0] * width))

    return pl.pallas_call(
        kernel,
        out_shape=(
            pltpu.VMEM((total, width), BF16),
            pltpu.VMEM((total, width), F32),
            pltpu.VMEM((depth - split, units), BF16),
        ),
        in_specs=[SMEM] + [VMEM] * (len(slots) + 1) + [HBM],
        out_specs=(VMEM,) * 3,
        scratch_shapes=[
            pltpu.VMEM((total, depth), BF16),
            pltpu.VMEM((total, units), F32),
            pltpu.SemaphoreType.DMA((parts,)),
        ],
        cost_estimate=cost(4 * total * depth * width, 2 * depth * width),
        compiler_params=params(26),
    )(info, *slots, upper, weight)


def join(parts):
    rows = sum(part.shape[0] for part in parts)

    def kernel(*refs):
        gathered_rows(refs[:-1], refs[-1])

    return pl.pallas_call(
        kernel,
        out_shape=pltpu.VMEM((rows, parts[0].shape[1]), parts[0].dtype),
        in_specs=[VMEM] * len(parts),
        out_specs=VMEM,
        cost_estimate=cost(0, 4 * rows * parts[0].shape[1]),
        compiler_params=params(1),
    )(*parts)


def product_tiles(tokens_ref, upper_ref, lower_ref, base, out_ref):
    split = upper_ref.shape[0]

    def body(down, col, tile):
        across = pl.ds(pl.multiple_of(base + col, 128), tile)
        product = jnp.dot(tokens_ref[down, :split], upper_ref[:, across], preferred_element_type=F32) + jnp.dot(
            tokens_ref[down, split:], lower_ref[:, across], preferred_element_type=F32
        )
        out_ref[down, pl.ds(col, tile)] = product.astype(out_ref.dtype)

    tiles(*out_ref.shape, 768, body)


def up_other(info, slots, upper, lower):
    depth = slots[0].shape[1]
    total = sum(slot.shape[0] for slot in slots)
    width = upper.shape[1] // 2

    def kernel(info_ref, *refs):
        upper_ref, lower_ref, out_ref, tokens_ref = refs[len(slots) :]
        gathered_rows(refs[: len(slots)], tokens_ref)
        product_tiles(tokens_ref, upper_ref, lower_ref, (1 - info_ref[0]) * width, out_ref)

    return pl.pallas_call(
        kernel,
        out_shape=(pltpu.VMEM((total, width), BF16), pltpu.VMEM((total, depth), BF16)),
        in_specs=[SMEM] + [VMEM] * (len(slots) + 2),
        out_specs=(VMEM, VMEM),
        cost_estimate=cost(2 * total * depth * width, 2 * depth * width),
        compiler_params=params(10),
    )(info, *slots, upper, lower)


def up_own(info, tokens, upper, lower):
    total, depth = tokens.shape
    width = upper.shape[1] // 2

    def kernel(info_ref, tokens_ref, upper_ref, lower_ref, out_ref):
        product_tiles(tokens_ref, upper_ref, lower_ref, info_ref[0] * width, out_ref)

    return pl.pallas_call(
        kernel,
        out_shape=pltpu.VMEM((total, width), F32),
        in_specs=[SMEM] + [VMEM] * 3,
        out_specs=VMEM,
        cost_estimate=cost(2 * total * depth * width, 2 * depth * width),
        compiler_params=params(10),
    )(info, tokens, upper, lower)


def gelu(value):
    return 0.5 * value * (1.0 + lax.erf(value * 0.7071067811865476))


def conv(info, own, received, up_bias, conv_weight, conv_bias, later, groups, links, rows, grid_y):
    width = own[0].shape[1]
    slots = [(group, index) + slot for group, members in enumerate(groups) for index, slot in enumerate(members)]
    blocks = len(slots)
    total = rows * blocks
    count = len(groups)
    lanes = 128
    extent_x = total // grid_y

    def kernel(info_ref, *refs):
        own_refs, received_refs = refs[:count], refs[count : 2 * count]
        up_bias_ref, weight_ref, bias_ref, later_ref, out_ref, later_out, hidden, sems = refs[2 * count :]
        copies = row_copies(later_ref, pl.multiple_of(info_ref[0] * width, 16), later_out, sems)
        for copy in copies:
            copy.start()
        hidden[0:grid_y, :] = jnp.zeros((grid_y, lanes), F32)
        hidden[(extent_x + 1) * grid_y : (extent_x + 2) * grid_y, :] = jnp.zeros((grid_y, lanes), F32)
        at_y = lax.broadcasted_iota(jnp.int32, (grid_y, lanes), 0)
        first, last = at_y == 0, at_y == grid_y - 1
        base = info_ref[0] * width
        places = [
            lax.rem(info_ref[1] + (links.ring - j), links.ring) * links.lanes + lax.rem(info_ref[2] + q, links.lanes)
            for _, _, q, j in slots
        ]

        def body(col, carry):
            across = pl.ds(pl.multiple_of(col * lanes, lanes), lanes)
            absolute = pl.ds(pl.multiple_of(base + col * lanes, lanes), lanes)
            shift = up_bias_ref[:, absolute]
            for slot in range(blocks):
                group, index, _, _ = slots[slot]
                down = slice(index * rows, (index + 1) * rows)
                value = own_refs[group][down, across] + received_refs[group][down, across].astype(F32) + shift
                target = pl.multiple_of(places[slot] * rows + grid_y, grid_y)
                hidden[pl.ds(target, rows), :] = value.astype(BF16).astype(F32)
            weights = [[weight_ref[a, b : b + 1, absolute] for b in range(3)] for a in range(3)]
            offset = bias_ref[:, absolute]
            for slot in range(blocks):
                for line in range(rows // grid_y):
                    start = places[slot] * rows + line * grid_y
                    near = [hidden[pl.ds(pl.multiple_of(start + a * grid_y, grid_y), grid_y), :] for a in range(3)]
                    sums = [near[0] * weights[0][b] + near[1] * weights[1][b] + near[2] * weights[2][b] for b in range(3)]
                    before = jnp.where(first, 0.0, pltpu.roll(sums[0], 1, axis=0))
                    after = jnp.where(last, 0.0, pltpu.roll(sums[2], grid_y - 1, axis=0))
                    value = sums[1] + before + after + offset
                    out_ref[slot * rows + line * grid_y : slot * rows + (line + 1) * grid_y, across] = gelu(value).astype(BF16)
            return carry

        lax.fori_loop(0, width // lanes, body, 0)
        for copy in copies:
            copy.wait()

    return pl.pallas_call(
        kernel,
        out_shape=(pltpu.VMEM((total, width), BF16), pltpu.VMEM((width, later.shape[1]), BF16)),
        in_specs=[SMEM] + [VMEM] * (2 * count + 3) + [HBM],
        out_specs=(VMEM, VMEM),
        scratch_shapes=[pltpu.VMEM(((extent_x + 2) * grid_y, lanes), F32), pltpu.SemaphoreType.DMA((4,))],
        cost_estimate=cost(60 * total * width, 8 * total * width),
        compiler_params=params(33),
    )(info, *own, *received, up_bias, conv_weight, conv_bias, later)


def down_own(info, mixed, weight, later):
    total, depth = mixed.shape
    width = weight.shape[1]
    tile = tile_of(width, 1024)
    high = tile_of(total, 256)

    def kernel(info_ref, mixed_ref, weight_ref, later_ref, out_ref, later_out, sems):
        copies = row_copies(later_ref, pl.multiple_of((1 - info_ref[0]) * depth, 16), later_out, sems)
        for copy in copies:
            copy.start()

        def body(step, carry):
            row, col = step // (width // tile), step % (width // tile)
            down = pl.ds(pl.multiple_of(row * high, high), high)
            across = pl.ds(pl.multiple_of(col * tile, tile), tile)
            out_ref[down, across] = jnp.dot(mixed_ref[down, :], weight_ref[:, across], preferred_element_type=F32)
            return carry

        lax.fori_loop(0, (total // high) * (width // tile), body, 0)
        for copy in copies:
            copy.wait()

    return pl.pallas_call(
        kernel,
        out_shape=(pltpu.VMEM((total, width), F32), pltpu.VMEM((depth, width), BF16)),
        in_specs=[SMEM] + [VMEM] * 2 + [HBM],
        out_specs=(VMEM, VMEM),
        scratch_shapes=[pltpu.SemaphoreType.DMA((4,))],
        cost_estimate=cost(2 * total * depth * width, 2 * depth * width),
        compiler_params=params(26),
    )(info, mixed, weight, later)


def down_other(mixed, weight, partial, first, outs):
    depth = mixed.shape[1]
    width = weight.shape[1]
    total = sum(rows for rows, _ in outs)
    tile = tile_of(width, 1024)

    def kernel(mixed_ref, weight_ref, partial_ref, *out_refs):
        def body(step, carry):
            across = pl.ds(pl.multiple_of(step * tile, tile), tile)
            start = 0
            pieces = []
            for out_ref in out_refs:
                rows = out_ref.shape[0]
                pieces.append((out_ref, start, rows))
                start += rows
            while pieces:
                take = 1
                while take < len(pieces) and sum(rows for _, _, rows in pieces[: take + 1]) <= 256:
                    take += 1
                low = pieces[0][1]
                high = sum(rows for _, _, rows in pieces[:take])
                down = slice(first + low, first + low + high)
                value = partial_ref[down, across] + jnp.dot(
                    mixed_ref[down, :], weight_ref[:, across], preferred_element_type=F32
                )
                for out_ref, at, rows in pieces[:take]:
                    out_ref[:, across] = value[at - low : at - low + rows].astype(out_ref.dtype)
                pieces = pieces[take:]
            return carry

        lax.fori_loop(0, width // tile, body, 0)

    return pl.pallas_call(
        kernel,
        out_shape=tuple(pltpu.VMEM((rows, width), kind) for rows, kind in outs),
        in_specs=[VMEM] * 3,
        out_specs=(VMEM,) * len(outs),
        cost_estimate=cost(2 * total * depth * width, 2 * depth * width),
        compiler_params=params(10),
    )(mixed, weight, partial)


def finish(info, totals, bias, cols, grid_half):
    width = totals[0].shape[1]
    half = width * len(totals)

    def kernel(info_ref, *refs):
        bias_ref, stay_ref, leave_ref = refs[len(totals) :]
        core = info_ref[0]
        for index in range(len(totals)):
            shift = bias_ref[:, pl.ds(pl.multiple_of(core * half + index * width, 128), width)]
            for col in range(cols):
                for out_ref, side in ((stay_ref, core), (leave_ref, 1 - core)):
                    source = pl.ds(pl.multiple_of((2 * col + side) * grid_half, 8), grid_half)
                    out_ref[col, :, index * width : (index + 1) * width] = (refs[index][source, :] + shift).astype(BF16)

    return pl.pallas_call(
        kernel,
        out_shape=(pltpu.VMEM((cols, grid_half, half), BF16),) * 2,
        in_specs=[SMEM] + [VMEM] * (len(totals) + 1),
        out_specs=(VMEM, VMEM),
        cost_estimate=cost(4 * cols * grid_half * half, 8 * cols * grid_half * half),
        compiler_params=params(4),
    )(info, *totals, bias)


def tie(*values):
    return lax.optimization_barrier(values)


class Links:
    def __init__(self, count):
        self.lanes = 2 if count % 2 == 0 else 1
        self.ring = count // self.lanes
        self.half = self.ring // 2
        self.upward = [(t, (t + self.lanes) % count) for t in range(count)]
        self.downward = [(t, s) for s, t in self.upward]
        self.pairs = [(t, t ^ 1) for t in range(count)]

    def up(self, value):
        return lax.ppermute(value, "tp", self.upward)

    def down(self, value):
        return lax.ppermute(value, "tp", self.downward)

    def cross(self, value):
        return lax.ppermute(value, "tp", self.pairs)


def gather(links, block, fetch_upper):
    column, beside = [block], []
    if links.lanes > 1:
        beside.append(links.cross(block))
    if links.half:
        column.append(links.up(block))
    upper = fetch_upper()
    start = block
    if links.lanes > 1:
        if links.half:
            upper, beside[0], column[1] = tie(upper, beside[0], column[1])
        if links.half + 1 < links.ring:
            start = join([block, beside[0]])
    for slot in range(1, links.half + 1):
        if slot > 1:
            column.append(links.up(column[slot - 1]))
        if links.lanes > 1:
            beside.append(links.cross(column[slot]))
    if links.half > 1 and links.half + 1 < links.ring:
        start, column[-1] = tie(start, column[-1])
    both = []
    for _ in range(links.half + 1, links.ring):
        start = links.down(start)
        both.append(start)
    early = column + beside[: links.half]
    late = beside[links.half :] + both
    names_early = [(0, j) for j in range(links.half + 1)] + [(1, j) for j in range(len(beside[: links.half]))]
    names_late = [(1, links.half)] * len(beside[links.half :])
    names_late += [(q, j) for j in range(links.ring - 1, links.half, -1) for q in range(links.lanes)]
    return early, late, [names_early] + ([names_late] if late else []), upper


def scatter(links, rows, names, late, early):
    ring, half = links.ring, links.half
    terms = {}

    def bring(make, members):
        terms.update(zip(members, make([(rows, BF16 if q else F32) for q, _ in members])))

    up_slots, down_slots = list(range(half + 1, ring)), list(range(half, 0, -1))
    order = [slot for both in zip(down_slots, up_slots) for slot in both]
    order += [slot for slot in down_slots + up_slots if slot not in order] + [0]
    crossed, arrived, ready = {}, {slot: [] for slot in range(ring)}, {}
    if len(names) > 1:
        bring(late, names[1])
    if links.lanes > 1 and half:
        crossed[half] = links.cross(terms[1, half])
    bring(early, names[0])
    if links.lanes > 1 and not half:
        crossed[0] = links.cross(terms[1, 0])
    for position, slot in enumerate(order):
        if links.lanes > 1 and position + 1 < ring:
            after = order[position + 1]
            if position == 0:
                terms[1, after], terms[0, 0] = tie(terms[1, after], terms[0, 0])
            else:
                before = order[position - 1]
                terms[1, after], ready[before] = tie(terms[1, after], ready[before])
            crossed[after] = links.cross(terms[1, after])
        total = terms[0, slot]
        for term in arrived[slot] + ([crossed[slot]] if links.lanes > 1 else []):
            total = total + term.astype(F32)
        if slot:
            ready[slot] = total.astype(BF16)
            if slot <= half:
                arrived[slot - 1].append(links.down(ready[slot]))
            else:
                arrived[(slot + 1) % ring].append(links.up(ready[slot]))
    return total


def local(tokens, up_weight, up_bias, conv_weight, conv_bias, down_weight, down_bias):
    cols, grid_half, width_model = tokens.shape
    half = width_model // 2
    part = half // 2
    units = up_weight.shape[1]
    units_half = units // 2
    grid_y = grid_half * 2
    rows = cols * grid_y

    links = Links(lax.axis_size("tp"))
    core = lax.axis_index("sp")
    mine = lax.axis_index("tp")
    swap = [(0, 1), (1, 0)]
    info = jnp.stack([core, mine // links.lanes, mine % links.lanes]).astype(jnp.int32)

    flat = tokens.reshape(cols * grid_half, width_model)
    keep = lax.dynamic_slice_in_dim(flat, core * half, half, axis=1)
    give = lax.dynamic_slice_in_dim(flat, (1 - core) * half, half, axis=1)
    take = lax.ppermute(give, "sp", swap)
    keep, take = (x.reshape(cols, 1, grid_half, half) for x in (keep, take))
    block = jnp.where(core == 0, jnp.concatenate([keep, take], 1), jnp.concatenate([take, keep], 1))
    block = block.reshape(rows, half)
    block, info = tie(block, info)

    early, late, groups, upper = gather(links, block, lambda: fetch(info, up_weight, lambda c: 0 * c, part, 0))

    early_other, early_own, lower = up_early(info, early, upper, up_weight)
    own, received = [early_own], [lax.ppermute(early_other, "sp", swap)]
    if late:
        late_other, late_tokens = up_other(info, late, upper, lower)
        received.append(lax.ppermute(late_other, "sp", swap))
        own.append(up_own(info, late_tokens, upper, lower))
    mixed, down_mine = conv(
        info,
        own,
        received,
        up_bias.reshape(1, units),
        conv_weight,
        conv_bias.reshape(1, units),
        down_weight,
        groups,
        links,
        rows,
        grid_y,
    )
    mixed_received = lax.ppermute(mixed, "sp", swap)
    product, down_theirs = down_own(info, mixed, down_mine, down_weight)

    early_rows = rows * len(groups[0])
    total = scatter(
        links,
        rows,
        groups,
        lambda outs: down_other(mixed_received, down_theirs, product, early_rows, outs),
        lambda outs: down_other(mixed_received, down_theirs, product, 0, outs),
    )

    stay, leave = finish(info, [total], down_bias.reshape(1, width_model), cols, grid_half)
    arrive = lax.ppermute(leave, "sp", swap)
    return jnp.where(core == 0, jnp.concatenate([stay, arrive], -1), jnp.concatenate([arrive, stay], -1))


def solution(mesh):
    placed = (
        P(("img", "tp"), "sp", None),
        P("sp", "tp"),
        P("tp"),
        P(None, None, "tp"),
        P("tp"),
        P("tp", "sp"),
        P(),
    )
    return jax.shard_map(
        local, mesh=mesh, in_specs=placed, out_specs=P(("img", "tp"), "sp", None), check_vma=False
    )
```

```python
import jax
import jax.numpy as jnp
from jax import lax
from jax.experimental import pallas as pl
from jax.experimental.pallas import tpu as pltpu
from jax.sharding import PartitionSpec as P

F32 = jnp.float32
BF16 = jnp.bfloat16
VMEM = pl.BlockSpec(memory_space=pltpu.VMEM)
HBM = pl.BlockSpec(memory_space=pltpu.HBM)
SMEM = pl.BlockSpec(memory_space=pltpu.SMEM)
MIB = 1 << 20
LIMITS = (24, 20, 36, 26)


def tile_of(size, most):
    for tile in range(most, 0, -128):
        if size % tile == 0:
            return tile
    return size


def cost(flops, moved, transcendentals=0):
    return pl.CostEstimate(flops=int(flops), bytes_accessed=int(moved), transcendentals=int(transcendentals))


def params(limit):
    return pltpu.CompilerParams(vmem_limit_bytes=limit * MIB)


def row_copies(weight_ref, first, out_ref, sems):
    parts = sems.shape[0]
    step = out_ref.shape[0] // parts
    return [
        pltpu.make_async_copy(
            weight_ref.at[pl.ds(first + part * step, step)], out_ref.at[pl.ds(part * step, step)], sems.at[part]
        )
        for part in range(parts)
    ]


def passengers(later, spans):
    shapes = [pltpu.VMEM((count, later.shape[1]), later.dtype) for _, _, count in spans]
    scratch = [pltpu.SemaphoreType.DMA((2,)) for _ in spans]
    units = later.shape[0] // 2

    def start(core, later_ref, out_refs, sem_refs):
        copies = []
        for (whose, first, _), out_ref, sems in zip(spans, out_refs, sem_refs):
            side = core if whose == 0 else 1 - core
            copies += row_copies(later_ref, pl.multiple_of(side * units + first, 16), out_ref, sems)
        for copy in copies:
            copy.start()
        return copies

    return shapes, scratch, start


def fetch(info, weight, start, count, held, parts=4):
    own_bytes = count * weight.shape[1] * 2
    limit = max(1, (60 * MIB - held - own_bytes) // MIB - 8)

    def kernel(info_ref, weight_ref, out_ref, sems):
        copies = row_copies(weight_ref, pl.multiple_of(start(info_ref[0]), 16), out_ref, sems)
        for copy in copies:
            copy.start()
        for copy in copies:
            copy.wait()

    return pl.pallas_call(
        kernel,
        out_shape=pltpu.VMEM((count, weight.shape[1]), weight.dtype),
        in_specs=[SMEM, HBM],
        out_specs=VMEM,
        scratch_shapes=[pltpu.SemaphoreType.DMA((parts,))],
        cost_estimate=cost(0, 2 * count * weight.shape[1] * 2),
        compiler_params=params(limit),
    )(info, weight)


def gathered_rows(slot_refs, tokens_ref):
    start = 0
    for ref in slot_refs:
        tokens_ref[start : start + ref.shape[0], :] = ref[...]
        start += ref.shape[0]


def tiles(total, width, most, body):
    tile = tile_of(width, most)
    high = tile_of(total, 256) if total > 256 else total

    def step_body(step, carry):
        row, col = step // (width // tile), step % (width // tile)
        body(pl.ds(pl.multiple_of(row * high, high), high), pl.multiple_of(col * tile, tile), tile)
        return carry

    lax.fori_loop(0, (total // high) * (width // tile), step_body, 0)


def up_early(info, slots, upper, weight):
    depth = slots[0].shape[1]
    total = sum(slot.shape[0] for slot in slots)
    split, units = upper.shape
    width = units // 2
    parts = 2
    step = (depth - split) // parts

    def kernel(info_ref, *refs):
        upper_ref, weight_ref, other_ref, own_ref, lower_ref, tokens_ref, sums_ref, sems = refs[len(slots) :]
        copies = row_copies(weight_ref, split, lower_ref, sems)
        for copy in copies:
            copy.start()
        gathered_rows(refs[: len(slots)], tokens_ref)

        def first(down, col, tile):
            across = pl.ds(col, tile)
            sums_ref[down, across] = jnp.dot(tokens_ref[down, :split], upper_ref[:, across], preferred_element_type=F32)

        tiles(total, units, 768, first)
        for part, copy in enumerate(copies):
            copy.wait()
            deep = slice(part * step, (part + 1) * step)
            features = slice(split + part * step, split + (part + 1) * step)

            def more(down, col, tile):
                across = pl.ds(col, tile)
                sums_ref[down, across] += jnp.dot(
                    tokens_ref[down, features], lower_ref[deep, across], preferred_element_type=F32
                )

            def last(out_ref, base):
                def body(down, col, tile):
                    across = pl.ds(pl.multiple_of(base + col, 128), tile)
                    value = sums_ref[down, across] + jnp.dot(
                        tokens_ref[down, features], lower_ref[deep, across], preferred_element_type=F32
                    )
                    out_ref[down, pl.ds(col, tile)] = value.astype(out_ref.dtype)

                return body

            if part < parts - 1:
                tiles(total, units, 768, more)
            else:
                tiles(total, width, 768, last(other_ref, (1 - info_ref[0]) * width))
                tiles(total, width, 768, last(own_ref, info_ref[0] * width))

    return pl.pallas_call(
        kernel,
        out_shape=(
            pltpu.VMEM((total, width), BF16),
            pltpu.VMEM((total, width), F32),
            pltpu.VMEM((depth - split, units), BF16),
        ),
        in_specs=[SMEM] + [VMEM] * (len(slots) + 1) + [HBM],
        out_specs=(VMEM,) * 3,
        scratch_shapes=[
            pltpu.VMEM((total, depth), BF16),
            pltpu.VMEM((total, units), F32),
            pltpu.SemaphoreType.DMA((parts,)),
        ],
        cost_estimate=cost(4 * total * depth * width, 2 * depth * width),
        compiler_params=params(26),
    )(info, *slots, upper, weight)


def join(parts):
    rows = sum(part.shape[0] for part in parts)

    def kernel(*refs):
        gathered_rows(refs[:-1], refs[-1])

    return pl.pallas_call(
        kernel,
        out_shape=pltpu.VMEM((rows, parts[0].shape[1]), parts[0].dtype),
        in_specs=[VMEM] * len(parts),
        out_specs=VMEM,
        cost_estimate=cost(0, 4 * rows * parts[0].shape[1]),
        compiler_params=params(1),
    )(*parts)


def product_tiles(tokens_ref, upper_ref, lower_ref, base, out_ref):
    split = upper_ref.shape[0]

    def body(down, col, tile):
        across = pl.ds(pl.multiple_of(base + col, 128), tile)
        product = jnp.dot(tokens_ref[down, :split], upper_ref[:, across], preferred_element_type=F32) + jnp.dot(
            tokens_ref[down, split:], lower_ref[:, across], preferred_element_type=F32
        )
        out_ref[down, pl.ds(col, tile)] = product.astype(out_ref.dtype)

    tiles(*out_ref.shape, 768, body)


def up_other(info, slots, upper, lower, later, spans):
    depth = slots[0].shape[1]
    total = sum(slot.shape[0] for slot in slots)
    width = upper.shape[1] // 2
    shapes, scratch, start = passengers(later, spans)

    def kernel(info_ref, *refs):
        upper_ref, lower_ref, later_ref, out_ref, tokens_ref = refs[len(slots) : len(slots) + 5]
        rest = refs[len(slots) + 5 :]
        copies = start(info_ref[0], later_ref, rest[: len(spans)], rest[len(spans) :])
        gathered_rows(refs[: len(slots)], tokens_ref)
        product_tiles(tokens_ref, upper_ref, lower_ref, (1 - info_ref[0]) * width, out_ref)
        for copy in copies:
            copy.wait()

    out, gathered, *pieces = pl.pallas_call(
        kernel,
        out_shape=(pltpu.VMEM((total, width), BF16), pltpu.VMEM((total, depth), BF16), *shapes),
        in_specs=[SMEM] + [VMEM] * (len(slots) + 2) + [HBM],
        out_specs=(VMEM,) * (2 + len(spans)),
        scratch_shapes=scratch,
        cost_estimate=cost(2 * total * depth * width, 2 * depth * width),
        compiler_params=params(LIMITS[0]),
    )(info, *slots, upper, lower, later)
    return out, gathered, pieces


def up_own(info, tokens, upper, lower, later, spans):
    total, depth = tokens.shape
    width = upper.shape[1] // 2
    shapes, scratch, start = passengers(later, spans)

    def kernel(info_ref, tokens_ref, upper_ref, lower_ref, later_ref, out_ref, *rest):
        copies = start(info_ref[0], later_ref, rest[: len(spans)], rest[len(spans) :])
        product_tiles(tokens_ref, upper_ref, lower_ref, info_ref[0] * width, out_ref)
        for copy in copies:
            copy.wait()

    out, *pieces = pl.pallas_call(
        kernel,
        out_shape=(pltpu.VMEM((total, width), F32), *shapes),
        in_specs=[SMEM] + [VMEM] * 3 + [HBM],
        out_specs=(VMEM,) * (1 + len(spans)),
        scratch_shapes=scratch,
        cost_estimate=cost(2 * total * depth * width, 2 * depth * width),
        compiler_params=params(LIMITS[1]),
    )(info, tokens, upper, lower, later)
    return out, pieces


def gelu(value):
    return 0.5 * value * (1.0 + lax.erf(value * 0.7071067811865476))


def conv(info, own, received, up_bias, conv_weight, conv_bias, later, spans, groups, links, rows, grid_y):
    width = own[0].shape[1]
    slots = [(group, index) + slot for group, members in enumerate(groups) for index, slot in enumerate(members)]
    blocks = len(slots)
    total = rows * blocks
    count = len(groups)
    lanes = 128
    extent_x = total // grid_y

    shapes, scratch, start_copies = passengers(later, spans)

    def kernel(info_ref, *refs):
        own_refs, received_refs = refs[:count], refs[count : 2 * count]
        up_bias_ref, weight_ref, bias_ref, later_ref, out_ref = refs[2 * count : 2 * count + 5]
        rest = refs[2 * count + 5 :]
        hidden = rest[len(spans)]
        copies = start_copies(info_ref[0], later_ref, rest[: len(spans)], rest[len(spans) + 1 :])
        hidden[0:grid_y, :] = jnp.zeros((grid_y, lanes), F32)
        hidden[(extent_x + 1) * grid_y : (extent_x + 2) * grid_y, :] = jnp.zeros((grid_y, lanes), F32)
        at_y = lax.broadcasted_iota(jnp.int32, (grid_y, lanes), 0)
        first, last = at_y == 0, at_y == grid_y - 1
        base = info_ref[0] * width
        places = [
            lax.rem(info_ref[1] + (links.ring - j), links.ring) * links.lanes + lax.rem(info_ref[2] + q, links.lanes)
            for _, _, q, j in slots
        ]

        def body(col, carry):
            across = pl.ds(pl.multiple_of(col * lanes, lanes), lanes)
            absolute = pl.ds(pl.multiple_of(base + col * lanes, lanes), lanes)
            shift = up_bias_ref[:, absolute]
            for slot in range(blocks):
                group, index, _, _ = slots[slot]
                down = slice(index * rows, (index + 1) * rows)
                value = own_refs[group][down, across] + received_refs[group][down, across].astype(F32) + shift
                target = pl.multiple_of(places[slot] * rows + grid_y, grid_y)
                hidden[pl.ds(target, rows), :] = value.astype(BF16).astype(F32)
            weights = [[weight_ref[a, b : b + 1, absolute] for b in range(3)] for a in range(3)]
            offset = bias_ref[:, absolute]
            for slot in range(blocks):
                for line in range(rows // grid_y):
                    start = places[slot] * rows + line * grid_y
                    near = [hidden[pl.ds(pl.multiple_of(start + a * grid_y, grid_y), grid_y), :] for a in range(3)]
                    sums = [near[0] * weights[0][b] + near[1] * weights[1][b] + near[2] * weights[2][b] for b in range(3)]
                    before = jnp.where(first, 0.0, pltpu.roll(sums[0], 1, axis=0))
                    after = jnp.where(last, 0.0, pltpu.roll(sums[2], grid_y - 1, axis=0))
                    value = sums[1] + before + after + offset
                    out_ref[slot * rows + line * grid_y : slot * rows + (line + 1) * grid_y, across] = gelu(value).astype(BF16)
            return carry

        lax.fori_loop(0, width // lanes, body, 0)
        for copy in copies:
            copy.wait()

    mixed, *pieces = pl.pallas_call(
        kernel,
        out_shape=(pltpu.VMEM((total, width), BF16), *shapes),
        in_specs=[SMEM] + [VMEM] * (2 * count + 3) + [HBM],
        out_specs=(VMEM,) * (1 + len(spans)),
        scratch_shapes=[pltpu.VMEM(((extent_x + 2) * grid_y, lanes), F32), *scratch],
        cost_estimate=cost(60 * total * width, 8 * total * width),
        compiler_params=params(LIMITS[2]),
    )(info, *own, *received, up_bias, conv_weight, conv_bias, later)
    return mixed, pieces


def dot_pieces(left_ref, down, piece_refs, across):
    value, start = None, 0
    for ref in piece_refs:
        deep = slice(start, start + ref.shape[0])
        term = jnp.dot(left_ref[down, deep], ref[:, across], preferred_element_type=F32)
        value = term if value is None else value + term
        start = deep.stop
    return value


def down_own(info, mixed, mine, later, spans):
    total, depth = mixed.shape
    width = later.shape[1]
    shapes, scratch, start = passengers(later, spans)

    def kernel(info_ref, mixed_ref, *refs):
        later_ref, out_ref = refs[len(mine) : len(mine) + 2]
        rest = refs[len(mine) + 2 :]
        copies = start(info_ref[0], later_ref, rest[: len(spans)], rest[len(spans) :])

        def body(down, col, tile):
            out_ref[down, pl.ds(col, tile)] = dot_pieces(mixed_ref, down, refs[: len(mine)], pl.ds(col, tile))

        tiles(total, width, 1024, body)
        for copy in copies:
            copy.wait()

    out, *pieces = pl.pallas_call(
        kernel,
        out_shape=(pltpu.VMEM((total, width), F32), *shapes),
        in_specs=[SMEM] + [VMEM] * (1 + len(mine)) + [HBM],
        out_specs=(VMEM,) * (1 + len(spans)),
        scratch_shapes=scratch,
        cost_estimate=cost(2 * total * depth * width, 2 * depth * width),
        compiler_params=params(LIMITS[3]),
    )(info, mixed, *mine, later)
    return out, pieces


def down_other(mixed, theirs, partial, first, outs):
    depth = mixed.shape[1]
    width = partial.shape[1]
    total = sum(rows for rows, _ in outs)
    tile = tile_of(width, 1024)

    runs, start = [], 0
    for index, (rows, _) in enumerate(outs):
        if not runs or runs[-1][1] + rows > 256:
            runs.append([start, 0, []])
        runs[-1][2].append((index, runs[-1][1], rows))
        runs[-1][1] += rows
        start += rows

    def kernel(mixed_ref, *refs):
        partial_ref, out_refs = refs[len(theirs)], refs[len(theirs) + 1 :]

        def body(step, carry):
            across = pl.ds(pl.multiple_of(step * tile, tile), tile)
            for low, high, members in runs:
                down = slice(first + low, first + low + high)
                value = partial_ref[down, across] + dot_pieces(mixed_ref, down, refs[: len(theirs)], across)
                for index, at, rows in members:
                    out_ref = out_refs[index]
                    out_ref[:, across] = value[at : at + rows].astype(out_ref.dtype)
            return carry

        lax.fori_loop(0, width // tile, body, 0)

    return pl.pallas_call(
        kernel,
        out_shape=tuple(pltpu.VMEM((rows, width), kind) for rows, kind in outs),
        in_specs=[VMEM] * (2 + len(theirs)),
        out_specs=(VMEM,) * len(outs),
        cost_estimate=cost(2 * total * depth * width, 2 * depth * width),
        compiler_params=params(10),
    )(mixed, *theirs, partial)


def finish(info, totals, bias, cols, grid_half):
    width = totals[0].shape[1]
    half = width * len(totals)

    def kernel(info_ref, *refs):
        bias_ref, stay_ref, leave_ref = refs[len(totals) :]
        core = info_ref[0]
        for index in range(len(totals)):
            shift = bias_ref[:, pl.ds(pl.multiple_of(core * half + index * width, 128), width)]
            for col in range(cols):
                for out_ref, side in ((stay_ref, core), (leave_ref, 1 - core)):
                    source = pl.ds(pl.multiple_of((2 * col + side) * grid_half, 8), grid_half)
                    out_ref[col, :, index * width : (index + 1) * width] = (refs[index][source, :] + shift).astype(BF16)

    return pl.pallas_call(
        kernel,
        out_shape=(pltpu.VMEM((cols, grid_half, half), BF16),) * 2,
        in_specs=[SMEM] + [VMEM] * (len(totals) + 1),
        out_specs=(VMEM, VMEM),
        cost_estimate=cost(4 * cols * grid_half * half, 8 * cols * grid_half * half),
        compiler_params=params(4),
    )(info, *totals, bias)


def tie(*values):
    return lax.optimization_barrier(values)


class Links:
    def __init__(self, count):
        self.lanes = 2 if count % 2 == 0 else 1
        self.ring = count // self.lanes
        self.half = self.ring // 2
        self.upward = [(t, (t + self.lanes) % count) for t in range(count)]
        self.downward = [(t, s) for s, t in self.upward]
        self.pairs = [(t, t ^ 1) for t in range(count)]

    def up(self, value):
        return lax.ppermute(value, "tp", self.upward)

    def down(self, value):
        return lax.ppermute(value, "tp", self.downward)

    def cross(self, value):
        return lax.ppermute(value, "tp", self.pairs)


def gather(links, block, fetch_upper):
    column, beside = [block], []
    if links.lanes > 1:
        beside.append(links.cross(block))
    if links.half:
        column.append(links.up(block))
    upper = fetch_upper()
    start = block
    if links.lanes > 1:
        if links.half:
            upper, beside[0], column[1] = tie(upper, beside[0], column[1])
        if links.half + 1 < links.ring:
            start = join([block, beside[0]])
    for slot in range(1, links.half + 1):
        if slot > 1:
            column.append(links.up(column[slot - 1]))
        if links.lanes > 1:
            beside.append(links.cross(column[slot]))
    if links.half > 1 and links.half + 1 < links.ring:
        start, column[-1] = tie(start, column[-1])
    both = []
    for _ in range(links.half + 1, links.ring):
        start = links.down(start)
        both.append(start)
    early = column + beside[: links.half]
    late = beside[links.half :] + both
    names_early = [(0, j) for j in range(links.half + 1)] + [(1, j) for j in range(len(beside[: links.half]))]
    names_late = [(1, links.half)] * len(beside[links.half :])
    names_late += [(q, j) for j in range(links.ring - 1, links.half, -1) for q in range(links.lanes)]
    return early, late, [names_early] + ([names_late] if late else []), upper


def scatter(links, rows, names, late, early):
    ring, half = links.ring, links.half
    terms = {}

    def bring(make, members):
        terms.update(zip(members, make([(rows, BF16 if q else F32) for q, _ in members])))

    up_slots, down_slots = list(range(half + 1, ring)), list(range(half, 0, -1))
    order = [slot for both in zip(down_slots, up_slots) for slot in both]
    order += [slot for slot in down_slots + up_slots if slot not in order] + [0]
    crossed, arrived, ready = {}, {slot: [] for slot in range(ring)}, {}
    if len(names) > 1:
        bring(late, names[1])
    if links.lanes > 1 and half:
        crossed[half] = links.cross(terms[1, half])
    bring(early, names[0])
    if links.lanes > 1 and not half:
        crossed[0] = links.cross(terms[1, 0])
    for position, slot in enumerate(order):
        if links.lanes > 1 and position + 1 < ring:
            after = order[position + 1]
            if position == 0:
                terms[1, after], terms[0, 0] = tie(terms[1, after], terms[0, 0])
            else:
                before = order[position - 1]
                terms[1, after], ready[before] = tie(terms[1, after], ready[before])
            crossed[after] = links.cross(terms[1, after])
        total = terms[0, slot]
        for term in arrived[slot] + ([crossed[slot]] if links.lanes > 1 else []):
            total = total + term.astype(F32)
        if slot:
            ready[slot] = total.astype(BF16)
            if slot <= half:
                arrived[slot - 1].append(links.down(ready[slot]))
            else:
                arrived[(slot + 1) % ring].append(links.up(ready[slot]))
    return total


def local(tokens, up_weight, up_bias, conv_weight, conv_bias, down_weight, down_bias):
    cols, grid_half, width_model = tokens.shape
    half = width_model // 2
    part = half // 2
    units = up_weight.shape[1]
    units_half = units // 2
    grid_y = grid_half * 2
    rows = cols * grid_y

    links = Links(lax.axis_size("tp"))
    core = lax.axis_index("sp")
    mine = lax.axis_index("tp")
    swap = [(0, 1), (1, 0)]
    info = jnp.stack([core, mine // links.lanes, mine % links.lanes]).astype(jnp.int32)

    flat = tokens.reshape(cols * grid_half, width_model)
    keep = lax.dynamic_slice_in_dim(flat, core * half, half, axis=1)
    give = lax.dynamic_slice_in_dim(flat, (1 - core) * half, half, axis=1)
    take = lax.ppermute(give, "sp", swap)
    keep, take = (x.reshape(cols, 1, grid_half, half) for x in (keep, take))
    block = jnp.where(core == 0, jnp.concatenate([keep, take], 1), jnp.concatenate([take, keep], 1))
    block = block.reshape(rows, half)
    block, info = tie(block, info)

    early, late, groups, upper = gather(links, block, lambda: fetch(info, up_weight, lambda c: 0 * c, part, 0))

    early_other, early_own, lower = up_early(info, early, upper, up_weight)
    third = units_half // 3 // 32 * 32
    rest = units_half - 2 * third
    late_other, late_tokens, mine_a = up_other(info, late, upper, lower, down_weight, [(0, 0, third)])
    late_own, mine_b = up_own(info, late_tokens, upper, lower, down_weight, [(0, third, third)])
    own = [early_own, late_own]
    received = [lax.ppermute(early_other, "sp", swap), lax.ppermute(late_other, "sp", swap)]
    mixed, (mine_c, theirs_a) = conv(
        info,
        own,
        received,
        up_bias.reshape(1, units),
        conv_weight,
        conv_bias.reshape(1, units),
        down_weight,
        [(0, 2 * third, rest), (1, 0, third)],
        groups,
        links,
        rows,
        grid_y,
    )
    mixed_received = lax.ppermute(mixed, "sp", swap)
    product, theirs_b = down_own(
        info, mixed, [*mine_a, *mine_b, mine_c], down_weight, [(1, third, units_half - third)]
    )
    theirs = [theirs_a, *theirs_b]

    early_rows = rows * len(groups[0])
    total = scatter(
        links,
        rows,
        groups,
        lambda outs: down_other(mixed_received, theirs, product, early_rows, outs),
        lambda outs: down_other(mixed_received, theirs, product, 0, outs),
    )

    stay, leave = finish(info, [total], down_bias.reshape(1, width_model), cols, grid_half)
    arrive = lax.ppermute(leave, "sp", swap)
    return jnp.where(core == 0, jnp.concatenate([stay, arrive], -1), jnp.concatenate([arrive, stay], -1))


def solution(mesh):
    placed = (
        P(("img", "tp"), "sp", None),
        P("sp", "tp"),
        P("tp"),
        P(None, None, "tp"),
        P("tp"),
        P("tp", "sp"),
        P(),
    )
    return jax.shard_map(
        local, mesh=mesh, in_specs=placed, out_specs=P(("img", "tp"), "sp", None), check_vma=False
    )
```

```python
import jax
import jax.numpy as jnp
from jax import lax
from jax.experimental import pallas as pl
from jax.experimental.pallas import tpu as pltpu
from jax.sharding import PartitionSpec as P

F32 = jnp.float32
BF16 = jnp.bfloat16
VMEM = pl.BlockSpec(memory_space=pltpu.VMEM)
HBM = pl.BlockSpec(memory_space=pltpu.HBM)
SMEM = pl.BlockSpec(memory_space=pltpu.SMEM)
MIB = 1 << 20
LIMITS = (24, 20, 36, 26)


def tile_of(size, most):
    for tile in range(most, 0, -128):
        if size % tile == 0:
            return tile
    return size


def cost(flops, moved, transcendentals=0):
    return pl.CostEstimate(flops=int(flops), bytes_accessed=int(moved), transcendentals=int(transcendentals))


def params(limit):
    return pltpu.CompilerParams(vmem_limit_bytes=limit * MIB)


def row_copies(weight_ref, first, out_ref, sems):
    parts = sems.shape[0]
    step = out_ref.shape[0] // parts
    return [
        pltpu.make_async_copy(
            weight_ref.at[pl.ds(first + part * step, step)], out_ref.at[pl.ds(part * step, step)], sems.at[part]
        )
        for part in range(parts)
    ]


def passengers(later, spans):
    shapes = [pltpu.VMEM((count, later.shape[1]), later.dtype) for _, _, count in spans]
    scratch = [pltpu.SemaphoreType.DMA((2,)) for _ in spans]
    units = later.shape[0] // 2

    def start(core, later_ref, out_refs, sem_refs):
        copies = []
        for (whose, first, _), out_ref, sems in zip(spans, out_refs, sem_refs):
            side = core if whose == 0 else 1 - core
            copies += row_copies(later_ref, pl.multiple_of(side * units + first, 16), out_ref, sems)
        for copy in copies:
            copy.start()
        return copies

    return shapes, scratch, start


def fetch(info, weight, start, count, held, parts=4):
    own_bytes = count * weight.shape[1] * 2
    limit = max(1, (60 * MIB - held - own_bytes) // MIB - 8)

    def kernel(info_ref, weight_ref, out_ref, sems):
        copies = row_copies(weight_ref, pl.multiple_of(start(info_ref[0]), 16), out_ref, sems)
        for copy in copies:
            copy.start()
        for copy in copies:
            copy.wait()

    return pl.pallas_call(
        kernel,
        out_shape=pltpu.VMEM((count, weight.shape[1]), weight.dtype),
        in_specs=[SMEM, HBM],
        out_specs=VMEM,
        scratch_shapes=[pltpu.SemaphoreType.DMA((parts,))],
        cost_estimate=cost(0, 2 * count * weight.shape[1] * 2),
        compiler_params=params(limit),
    )(info, weight)


def gathered_rows(slot_refs, tokens_ref):
    start = 0
    for ref in slot_refs:
        tokens_ref[start : start + ref.shape[0], :] = ref[...]
        start += ref.shape[0]


def tiles(total, width, most, body):
    tile = tile_of(width, most)
    high = tile_of(total, 256) if total > 256 else total

    def step_body(step, carry):
        row, col = step // (width // tile), step % (width // tile)
        body(pl.ds(pl.multiple_of(row * high, high), high), pl.multiple_of(col * tile, tile), tile)
        return carry

    lax.fori_loop(0, (total // high) * (width // tile), step_body, 0)


def up_early(info, slots, upper, weight):
    depth = slots[0].shape[1]
    total = sum(slot.shape[0] for slot in slots)
    split, units = upper.shape
    width = units // 2
    parts = 2
    step = (depth - split) // parts

    def kernel(info_ref, *refs):
        upper_ref, weight_ref, other_ref, own_ref, lower_ref, tokens_ref, sums_ref, sems = refs[len(slots) :]
        copies = row_copies(weight_ref, split, lower_ref, sems)
        for copy in copies:
            copy.start()
        gathered_rows(refs[: len(slots)], tokens_ref)

        def first(down, col, tile):
            across = pl.ds(col, tile)
            sums_ref[down, across] = jnp.dot(tokens_ref[down, :split], upper_ref[:, across], preferred_element_type=F32)

        tiles(total, units, 768, first)
        for part, copy in enumerate(copies):
            copy.wait()
            deep = slice(part * step, (part + 1) * step)
            features = slice(split + part * step, split + (part + 1) * step)

            def more(down, col, tile):
                across = pl.ds(col, tile)
                sums_ref[down, across] += jnp.dot(
                    tokens_ref[down, features], lower_ref[deep, across], preferred_element_type=F32
                )

            def last(out_ref, base):
                def body(down, col, tile):
                    across = pl.ds(pl.multiple_of(base + col, 128), tile)
                    value = sums_ref[down, across] + jnp.dot(
                        tokens_ref[down, features], lower_ref[deep, across], preferred_element_type=F32
                    )
                    out_ref[down, pl.ds(col, tile)] = value.astype(out_ref.dtype)

                return body

            if part < parts - 1:
                tiles(total, units, 768, more)
            else:
                tiles(total, width, 768, last(other_ref, (1 - info_ref[0]) * width))
                tiles(total, width, 768, last(own_ref, info_ref[0] * width))

    return pl.pallas_call(
        kernel,
        out_shape=(
            pltpu.VMEM((total, width), BF16),
            pltpu.VMEM((total, width), F32),
            pltpu.VMEM((depth - split, units), BF16),
        ),
        in_specs=[SMEM] + [VMEM] * (len(slots) + 1) + [HBM],
        out_specs=(VMEM,) * 3,
        scratch_shapes=[
            pltpu.VMEM((total, depth), BF16),
            pltpu.VMEM((total, units), F32),
            pltpu.SemaphoreType.DMA((parts,)),
        ],
        cost_estimate=cost(4 * total * depth * width, 2 * depth * width),
        compiler_params=params(26),
    )(info, *slots, upper, weight)


def join(parts):
    rows = sum(part.shape[0] for part in parts)

    def kernel(*refs):
        gathered_rows(refs[:-1], refs[-1])

    return pl.pallas_call(
        kernel,
        out_shape=pltpu.VMEM((rows, parts[0].shape[1]), parts[0].dtype),
        in_specs=[VMEM] * len(parts),
        out_specs=VMEM,
        cost_estimate=cost(0, 4 * rows * parts[0].shape[1]),
        compiler_params=params(1),
    )(*parts)


def product_tiles(tokens_ref, upper_ref, lower_ref, base, out_ref):
    split = upper_ref.shape[0]

    def body(down, col, tile):
        across = pl.ds(pl.multiple_of(base + col, 128), tile)
        product = jnp.dot(tokens_ref[down, :split], upper_ref[:, across], preferred_element_type=F32) + jnp.dot(
            tokens_ref[down, split:], lower_ref[:, across], preferred_element_type=F32
        )
        out_ref[down, pl.ds(col, tile)] = product.astype(out_ref.dtype)

    tiles(*out_ref.shape, 768, body)


def up_other(info, slots, upper, lower, later, spans):
    depth = slots[0].shape[1]
    total = sum(slot.shape[0] for slot in slots)
    width = upper.shape[1] // 2
    shapes, scratch, start = passengers(later, spans)

    def kernel(info_ref, *refs):
        upper_ref, lower_ref, later_ref, out_ref, tokens_ref = refs[len(slots) : len(slots) + 5]
        rest = refs[len(slots) + 5 :]
        copies = start(info_ref[0], later_ref, rest[: len(spans)], rest[len(spans) :])
        gathered_rows(refs[: len(slots)], tokens_ref)
        product_tiles(tokens_ref, upper_ref, lower_ref, (1 - info_ref[0]) * width, out_ref)
        for copy in copies:
            copy.wait()

    out, gathered, *pieces = pl.pallas_call(
        kernel,
        out_shape=(pltpu.VMEM((total, width), BF16), pltpu.VMEM((total, depth), BF16), *shapes),
        in_specs=[SMEM] + [VMEM] * (len(slots) + 2) + [HBM],
        out_specs=(VMEM,) * (2 + len(spans)),
        scratch_shapes=scratch,
        cost_estimate=cost(2 * total * depth * width, 2 * depth * width),
        compiler_params=params(LIMITS[0]),
    )(info, *slots, upper, lower, later)
    return out, gathered, pieces


def up_own(info, tokens, upper, lower, later, spans):
    total, depth = tokens.shape
    width = upper.shape[1] // 2
    shapes, scratch, start = passengers(later, spans)

    def kernel(info_ref, tokens_ref, upper_ref, lower_ref, later_ref, out_ref, *rest):
        copies = start(info_ref[0], later_ref, rest[: len(spans)], rest[len(spans) :])
        product_tiles(tokens_ref, upper_ref, lower_ref, info_ref[0] * width, out_ref)
        for copy in copies:
            copy.wait()

    out, *pieces = pl.pallas_call(
        kernel,
        out_shape=(pltpu.VMEM((total, width), F32), *shapes),
        in_specs=[SMEM] + [VMEM] * 3 + [HBM],
        out_specs=(VMEM,) * (1 + len(spans)),
        scratch_shapes=scratch,
        cost_estimate=cost(2 * total * depth * width, 2 * depth * width),
        compiler_params=params(LIMITS[1]),
    )(info, tokens, upper, lower, later)
    return out, pieces


def gelu(value):
    return 0.5 * value * (1.0 + lax.erf(value * 0.7071067811865476))


def conv(info, own, received, up_bias, conv_weight, conv_bias, later, spans, groups, links, rows, grid_y):
    width = own[0].shape[1]
    slots = [(group, index) + slot for group, members in enumerate(groups) for index, slot in enumerate(members)]
    blocks = len(slots)
    total = rows * blocks
    count = len(groups)
    lanes = 128
    extent_x = total // grid_y

    shapes, scratch, start_copies = passengers(later, spans)

    def kernel(info_ref, *refs):
        own_refs, received_refs = refs[:count], refs[count : 2 * count]
        up_bias_ref, weight_ref, bias_ref, later_ref, out_ref = refs[2 * count : 2 * count + 5]
        rest = refs[2 * count + 5 :]
        hidden = rest[len(spans)]
        copies = start_copies(info_ref[0], later_ref, rest[: len(spans)], rest[len(spans) + 1 :])
        hidden[0:grid_y, :] = jnp.zeros((grid_y, lanes), F32)
        hidden[(extent_x + 1) * grid_y : (extent_x + 2) * grid_y, :] = jnp.zeros((grid_y, lanes), F32)
        at_y = lax.broadcasted_iota(jnp.int32, (grid_y, lanes), 0)
        first, last = at_y == 0, at_y == grid_y - 1
        base = info_ref[0] * width
        places = [
            links.swapped(lax.rem(info_ref[1] + (links.ring - j), links.ring)) * links.lanes
            + lax.rem(info_ref[2] + q, links.lanes)
            for _, _, q, j in slots
        ]

        def body(col, carry):
            across = pl.ds(pl.multiple_of(col * lanes, lanes), lanes)
            absolute = pl.ds(pl.multiple_of(base + col * lanes, lanes), lanes)
            shift = up_bias_ref[:, absolute]
            for slot in range(blocks):
                group, index, _, _ = slots[slot]
                down = slice(index * rows, (index + 1) * rows)
                value = own_refs[group][down, across] + received_refs[group][down, across].astype(F32) + shift
                target = pl.multiple_of(places[slot] * rows + grid_y, grid_y)
                hidden[pl.ds(target, rows), :] = value.astype(BF16).astype(F32)
            weights = [[weight_ref[a, b : b + 1, absolute] for b in range(3)] for a in range(3)]
            offset = bias_ref[:, absolute]
            for slot in range(blocks):
                for line in range(rows // grid_y):
                    start = places[slot] * rows + line * grid_y
                    near = [hidden[pl.ds(pl.multiple_of(start + a * grid_y, grid_y), grid_y), :] for a in range(3)]
                    sums = [near[0] * weights[0][b] + near[1] * weights[1][b] + near[2] * weights[2][b] for b in range(3)]
                    before = jnp.where(first, 0.0, pltpu.roll(sums[0], 1, axis=0))
                    after = jnp.where(last, 0.0, pltpu.roll(sums[2], grid_y - 1, axis=0))
                    value = sums[1] + before + after + offset
                    out_ref[slot * rows + line * grid_y : slot * rows + (line + 1) * grid_y, across] = gelu(value).astype(BF16)
            return carry

        lax.fori_loop(0, width // lanes, body, 0)
        for copy in copies:
            copy.wait()

    mixed, *pieces = pl.pallas_call(
        kernel,
        out_shape=(pltpu.VMEM((total, width), BF16), *shapes),
        in_specs=[SMEM] + [VMEM] * (2 * count + 3) + [HBM],
        out_specs=(VMEM,) * (1 + len(spans)),
        scratch_shapes=[pltpu.VMEM(((extent_x + 2) * grid_y, lanes), F32), *scratch],
        cost_estimate=cost(60 * total * width, 8 * total * width),
        compiler_params=params(LIMITS[2]),
    )(info, *own, *received, up_bias, conv_weight, conv_bias, later)
    return mixed, pieces


def dot_pieces(left_ref, down, piece_refs, across):
    value, start = None, 0
    for ref in piece_refs:
        deep = slice(start, start + ref.shape[0])
        term = jnp.dot(left_ref[down, deep], ref[:, across], preferred_element_type=F32)
        value = term if value is None else value + term
        start = deep.stop
    return value


def down_own(info, mixed, mine, later, spans):
    total, depth = mixed.shape
    width = later.shape[1]
    shapes, scratch, start = passengers(later, spans)

    def kernel(info_ref, mixed_ref, *refs):
        later_ref, out_ref = refs[len(mine) : len(mine) + 2]
        rest = refs[len(mine) + 2 :]
        copies = start(info_ref[0], later_ref, rest[: len(spans)], rest[len(spans) :])

        def body(down, col, tile):
            out_ref[down, pl.ds(col, tile)] = dot_pieces(mixed_ref, down, refs[: len(mine)], pl.ds(col, tile))

        tiles(total, width, 1024, body)
        for copy in copies:
            copy.wait()

    out, *pieces = pl.pallas_call(
        kernel,
        out_shape=(pltpu.VMEM((total, width), F32), *shapes),
        in_specs=[SMEM] + [VMEM] * (1 + len(mine)) + [HBM],
        out_specs=(VMEM,) * (1 + len(spans)),
        scratch_shapes=scratch,
        cost_estimate=cost(2 * total * depth * width, 2 * depth * width),
        compiler_params=params(LIMITS[3]),
    )(info, mixed, *mine, later)
    return out, pieces


def down_other(mixed, theirs, partial, first, outs):
    depth = mixed.shape[1]
    width = partial.shape[1]
    total = sum(rows for rows, _ in outs)
    tile = tile_of(width, 1024)

    runs, start = [], 0
    for index, (rows, _) in enumerate(outs):
        if not runs or runs[-1][1] + rows > 256:
            runs.append([start, 0, []])
        runs[-1][2].append((index, runs[-1][1], rows))
        runs[-1][1] += rows
        start += rows

    def kernel(mixed_ref, *refs):
        partial_ref, out_refs = refs[len(theirs)], refs[len(theirs) + 1 :]

        def body(step, carry):
            across = pl.ds(pl.multiple_of(step * tile, tile), tile)
            for low, high, members in runs:
                down = slice(first + low, first + low + high)
                value = partial_ref[down, across] + dot_pieces(mixed_ref, down, refs[: len(theirs)], across)
                for index, at, rows in members:
                    out_ref = out_refs[index]
                    out_ref[:, across] = value[at : at + rows].astype(out_ref.dtype)
            return carry

        lax.fori_loop(0, width // tile, body, 0)

    return pl.pallas_call(
        kernel,
        out_shape=tuple(pltpu.VMEM((rows, width), kind) for rows, kind in outs),
        in_specs=[VMEM] * (2 + len(theirs)),
        out_specs=(VMEM,) * len(outs),
        cost_estimate=cost(2 * total * depth * width, 2 * depth * width),
        compiler_params=params(10),
    )(mixed, *theirs, partial)


def finish(info, totals, bias, cols, grid_half):
    width = totals[0].shape[1]
    half = width * len(totals)

    def kernel(info_ref, *refs):
        bias_ref, stay_ref, leave_ref = refs[len(totals) :]
        core = info_ref[0]
        for index in range(len(totals)):
            shift = bias_ref[:, pl.ds(pl.multiple_of(core * half + index * width, 128), width)]
            for col in range(cols):
                for out_ref, side in ((stay_ref, core), (leave_ref, 1 - core)):
                    source = pl.ds(pl.multiple_of((2 * col + side) * grid_half, 8), grid_half)
                    out_ref[col, :, index * width : (index + 1) * width] = (refs[index][source, :] + shift).astype(BF16)

    return pl.pallas_call(
        kernel,
        out_shape=(pltpu.VMEM((cols, grid_half, half), BF16),) * 2,
        in_specs=[SMEM] + [VMEM] * (len(totals) + 1),
        out_specs=(VMEM, VMEM),
        cost_estimate=cost(4 * cols * grid_half * half, 8 * cols * grid_half * half),
        compiler_params=params(4),
    )(info, *totals, bias)


def tie(*values):
    return lax.optimization_barrier(values)


class Links:
    def __init__(self, count):
        self.lanes = 2 if count % 2 == 0 else 1
        self.ring = count // self.lanes
        self.half = self.ring // 2
        self.upward = []
        for t in range(count):
            onward = self.swapped((self.swapped(t // self.lanes) + 1) % self.ring)
            self.upward.append((t, onward * self.lanes + t % self.lanes))
        self.downward = [(t, s) for s, t in self.upward]
        self.pairs = [(t, t ^ 1) for t in range(count)]

    def swapped(self, place):
        return place ^ (place >> 1) if self.ring == 4 else place

    def up(self, value):
        return lax.ppermute(value, "tp", self.upward)

    def down(self, value):
        return lax.ppermute(value, "tp", self.downward)

    def cross(self, value):
        return lax.ppermute(value, "tp", self.pairs)


def gather(links, block, fetch_upper):
    column, beside = [block], []
    if links.lanes > 1:
        beside.append(links.cross(block))
    if links.half:
        column.append(links.up(block))
    upper = fetch_upper()
    start = block
    if links.lanes > 1:
        if links.half:
            upper, beside[0], column[1] = tie(upper, beside[0], column[1])
        if links.half + 1 < links.ring:
            start = join([block, beside[0]])
    for slot in range(1, links.half + 1):
        if slot > 1:
            column.append(links.up(column[slot - 1]))
        if links.lanes > 1:
            beside.append(links.cross(column[slot]))
    if links.half > 1 and links.half + 1 < links.ring:
        start, column[-1] = tie(start, column[-1])
    both = []
    for _ in range(links.half + 1, links.ring):
        start = links.down(start)
        both.append(start)
    early = column + beside[: links.half]
    late = beside[links.half :] + both
    names_early = [(0, j) for j in range(links.half + 1)] + [(1, j) for j in range(len(beside[: links.half]))]
    names_late = [(1, links.half)] * len(beside[links.half :])
    names_late += [(q, j) for j in range(links.ring - 1, links.half, -1) for q in range(links.lanes)]
    return early, late, [names_early] + ([names_late] if late else []), upper


def scatter(links, rows, names, late, early):
    ring, half = links.ring, links.half
    terms = {}

    def bring(make, members):
        terms.update(zip(members, make([(rows, BF16 if q else F32) for q, _ in members])))

    up_slots, down_slots = list(range(half + 1, ring)), list(range(half, 0, -1))
    order = [slot for both in zip(down_slots, up_slots) for slot in both]
    order += [slot for slot in down_slots + up_slots if slot not in order] + [0]
    crossed, arrived, ready = {}, {slot: [] for slot in range(ring)}, {}
    if len(names) > 1:
        bring(late, names[1])
    if links.lanes > 1 and half:
        crossed[half] = links.cross(terms[1, half])
    bring(early, names[0])
    if links.lanes > 1 and not half:
        crossed[0] = links.cross(terms[1, 0])
    for position, slot in enumerate(order):
        if links.lanes > 1 and position + 1 < ring:
            after = order[position + 1]
            if position == 0:
                terms[1, after], terms[0, 0] = tie(terms[1, after], terms[0, 0])
            else:
                before = order[position - 1]
                terms[1, after], ready[before] = tie(terms[1, after], ready[before])
            crossed[after] = links.cross(terms[1, after])
        total = terms[0, slot]
        for term in arrived[slot] + ([crossed[slot]] if links.lanes > 1 else []):
            total = total + term.astype(F32)
        if slot:
            ready[slot] = total.astype(BF16)
            if slot <= half:
                arrived[slot - 1].append(links.down(ready[slot]))
            else:
                arrived[(slot + 1) % ring].append(links.up(ready[slot]))
    return total


def local(tokens, up_weight, up_bias, conv_weight, conv_bias, down_weight, down_bias):
    cols, grid_half, width_model = tokens.shape
    half = width_model // 2
    part = half // 2
    units = up_weight.shape[1]
    units_half = units // 2
    grid_y = grid_half * 2
    rows = cols * grid_y

    links = Links(lax.axis_size("tp"))
    core = lax.axis_index("sp")
    mine = lax.axis_index("tp")
    swap = [(0, 1), (1, 0)]
    info = jnp.stack([core, links.swapped(mine // links.lanes), mine % links.lanes]).astype(jnp.int32)

    flat = tokens.reshape(cols * grid_half, width_model)
    whole = lax.ppermute(flat, "sp", swap)
    keep = lax.dynamic_slice_in_dim(flat, core * half, half, axis=1)
    take = lax.dynamic_slice_in_dim(whole, core * half, half, axis=1)
    keep, take = (x.reshape(cols, 1, grid_half, half) for x in (keep, take))
    block = jnp.where(core == 0, jnp.concatenate([keep, take], 1), jnp.concatenate([take, keep], 1))
    block = block.reshape(rows, half)
    block, info = tie(block, info)

    early, late, groups, upper = gather(links, block, lambda: fetch(info, up_weight, lambda c: 0 * c, part, 0))

    early_other, early_own, lower = up_early(info, early, upper, up_weight)
    third = units_half // 3 // 32 * 32
    rest = units_half - 2 * third
    late_other, late_tokens, mine_a = up_other(info, late, upper, lower, down_weight, [(0, 0, third)])
    late_own, mine_b = up_own(info, late_tokens, upper, lower, down_weight, [(0, third, third)])
    own = [early_own, late_own]
    received = [lax.ppermute(early_other, "sp", swap), lax.ppermute(late_other, "sp", swap)]
    mixed, (mine_c, theirs_a) = conv(
        info,
        own,
        received,
        up_bias.reshape(1, units),
        conv_weight,
        conv_bias.reshape(1, units),
        down_weight,
        [(0, 2 * third, rest), (1, 0, third)],
        groups,
        links,
        rows,
        grid_y,
    )
    mixed_received = lax.ppermute(mixed, "sp", swap)
    product, theirs_b = down_own(
        info, mixed, [*mine_a, *mine_b, mine_c], down_weight, [(1, third, units_half - third)]
    )
    theirs = [theirs_a, *theirs_b]

    early_rows = rows * len(groups[0])
    total = scatter(
        links,
        rows,
        groups,
        lambda outs: down_other(mixed_received, theirs, product, early_rows, outs),
        lambda outs: down_other(mixed_received, theirs, product, 0, outs),
    )

    stay, leave = finish(info, [total], down_bias.reshape(1, width_model), cols, grid_half)
    arrive = lax.ppermute(leave, "sp", swap)
    return jnp.where(core == 0, jnp.concatenate([stay, arrive], -1), jnp.concatenate([arrive, stay], -1))


def solution(mesh):
    placed = (
        P(("img", "tp"), "sp", None),
        P("sp", "tp"),
        P("tp"),
        P(None, None, "tp"),
        P("tp"),
        P("tp", "sp"),
        P(),
    )
    return jax.shard_map(
        local, mesh=mesh, in_specs=placed, out_specs=P(("img", "tp"), "sp", None), check_vma=False
    )
```

```python
import jax
import jax.numpy as jnp
from jax import lax
from jax.experimental import pallas as pl
from jax.experimental.pallas import tpu as pltpu
from jax.sharding import PartitionSpec as P

F32 = jnp.float32
BF16 = jnp.bfloat16
VMEM = pl.BlockSpec(memory_space=pltpu.VMEM)
HBM = pl.BlockSpec(memory_space=pltpu.HBM)
SMEM = pl.BlockSpec(memory_space=pltpu.SMEM)
MIB = 1 << 20
LIMITS = (24, 20, 36, 26)


def tile_of(size, most):
    for tile in range(most, 0, -128):
        if size % tile == 0:
            return tile
    return size


def cost(flops, moved, transcendentals=0):
    return pl.CostEstimate(flops=int(flops), bytes_accessed=int(moved), transcendentals=int(transcendentals))


def params(limit):
    return pltpu.CompilerParams(vmem_limit_bytes=limit * MIB)


def row_copies(weight_ref, first, out_ref, sems):
    parts = sems.shape[0]
    step = out_ref.shape[0] // parts
    return [
        pltpu.make_async_copy(
            weight_ref.at[pl.ds(first + part * step, step)], out_ref.at[pl.ds(part * step, step)], sems.at[part]
        )
        for part in range(parts)
    ]


def passengers(later, spans):
    shapes = [pltpu.VMEM((count, later.shape[1]), later.dtype) for _, _, count in spans]
    scratch = [pltpu.SemaphoreType.DMA((2,)) for _ in spans]
    units = later.shape[0] // 2

    def start(core, later_ref, out_refs, sem_refs):
        copies = []
        for (whose, first, _), out_ref, sems in zip(spans, out_refs, sem_refs):
            side = core if whose == 0 else 1 - core
            copies += row_copies(later_ref, pl.multiple_of(side * units + first, 16), out_ref, sems)
        for copy in copies:
            copy.start()
        return copies

    return shapes, scratch, start


def fetch(info, weight, start, count, held, parts=4):
    own_bytes = count * weight.shape[1] * 2
    limit = max(1, (60 * MIB - held - own_bytes) // MIB - 8)

    def kernel(info_ref, weight_ref, out_ref, sems):
        copies = row_copies(weight_ref, pl.multiple_of(start(info_ref[0]), 16), out_ref, sems)
        for copy in copies:
            copy.start()
        for copy in copies:
            copy.wait()

    return pl.pallas_call(
        kernel,
        out_shape=pltpu.VMEM((count, weight.shape[1]), weight.dtype),
        in_specs=[SMEM, HBM],
        out_specs=VMEM,
        scratch_shapes=[pltpu.SemaphoreType.DMA((parts,))],
        cost_estimate=cost(0, 2 * count * weight.shape[1] * 2),
        compiler_params=params(limit),
    )(info, weight)


def gathered_rows(slot_refs, tokens_ref):
    start = 0
    for ref in slot_refs:
        tokens_ref[start : start + ref.shape[0], :] = ref[...]
        start += ref.shape[0]


def tiles(total, width, most, body):
    tile = tile_of(width, most)
    high = tile_of(total, 256) if total > 256 else total

    def step_body(step, carry):
        row, col = step // (width // tile), step % (width // tile)
        body(pl.ds(pl.multiple_of(row * high, high), high), pl.multiple_of(col * tile, tile), tile)
        return carry

    lax.fori_loop(0, (total // high) * (width // tile), step_body, 0)


def up_early(info, slots, upper, weight):
    depth = slots[0].shape[1]
    total = sum(slot.shape[0] for slot in slots)
    split, units = upper.shape
    width = units // 2
    parts = 2
    step = (depth - split) // parts

    def kernel(info_ref, *refs):
        upper_ref, weight_ref, other_ref, own_ref, lower_ref, tokens_ref, sums_ref, sems = refs[len(slots) :]
        copies = row_copies(weight_ref, split, lower_ref, sems)
        for copy in copies:
            copy.start()
        gathered_rows(refs[: len(slots)], tokens_ref)

        def first(down, col, tile):
            across = pl.ds(col, tile)
            sums_ref[down, across] = jnp.dot(tokens_ref[down, :split], upper_ref[:, across], preferred_element_type=F32)

        tiles(total, units, 768, first)
        for part, copy in enumerate(copies):
            copy.wait()
            deep = slice(part * step, (part + 1) * step)
            features = slice(split + part * step, split + (part + 1) * step)

            def more(down, col, tile):
                across = pl.ds(col, tile)
                sums_ref[down, across] += jnp.dot(
                    tokens_ref[down, features], lower_ref[deep, across], preferred_element_type=F32
                )

            def last(out_ref, base):
                def body(down, col, tile):
                    across = pl.ds(pl.multiple_of(base + col, 128), tile)
                    value = sums_ref[down, across] + jnp.dot(
                        tokens_ref[down, features], lower_ref[deep, across], preferred_element_type=F32
                    )
                    out_ref[down, pl.ds(col, tile)] = value.astype(out_ref.dtype)

                return body

            if part < parts - 1:
                tiles(total, units, 768, more)
            else:
                tiles(total, width, 768, last(other_ref, (1 - info_ref[0]) * width))
                tiles(total, width, 768, last(own_ref, info_ref[0] * width))

    return pl.pallas_call(
        kernel,
        out_shape=(
            pltpu.VMEM((total, width), BF16),
            pltpu.VMEM((total, width), F32),
            pltpu.VMEM((depth - split, units), BF16),
        ),
        in_specs=[SMEM] + [VMEM] * (len(slots) + 1) + [HBM],
        out_specs=(VMEM,) * 3,
        scratch_shapes=[
            pltpu.VMEM((total, depth), BF16),
            pltpu.VMEM((total, units), F32),
            pltpu.SemaphoreType.DMA((parts,)),
        ],
        cost_estimate=cost(4 * total * depth * width, 2 * depth * width),
        compiler_params=params(26),
    )(info, *slots, upper, weight)


def join(parts):
    rows = sum(part.shape[0] for part in parts)

    def kernel(*refs):
        gathered_rows(refs[:-1], refs[-1])

    return pl.pallas_call(
        kernel,
        out_shape=pltpu.VMEM((rows, parts[0].shape[1]), parts[0].dtype),
        in_specs=[VMEM] * len(parts),
        out_specs=VMEM,
        cost_estimate=cost(0, 4 * rows * parts[0].shape[1]),
        compiler_params=params(1),
    )(*parts)


def product_tiles(tokens_ref, upper_ref, lower_ref, base, out_ref):
    split = upper_ref.shape[0]

    def body(down, col, tile):
        across = pl.ds(pl.multiple_of(base + col, 128), tile)
        product = jnp.dot(tokens_ref[down, :split], upper_ref[:, across], preferred_element_type=F32) + jnp.dot(
            tokens_ref[down, split:], lower_ref[:, across], preferred_element_type=F32
        )
        out_ref[down, pl.ds(col, tile)] = product.astype(out_ref.dtype)

    tiles(*out_ref.shape, 768, body)


def up_other(info, slots, upper, lower, later, spans):
    depth = slots[0].shape[1]
    total = sum(slot.shape[0] for slot in slots)
    width = upper.shape[1] // 2
    shapes, scratch, start = passengers(later, spans)

    def kernel(info_ref, *refs):
        upper_ref, lower_ref, later_ref, out_ref, tokens_ref = refs[len(slots) : len(slots) + 5]
        rest = refs[len(slots) + 5 :]
        copies = start(info_ref[0], later_ref, rest[: len(spans)], rest[len(spans) :])
        gathered_rows(refs[: len(slots)], tokens_ref)
        product_tiles(tokens_ref, upper_ref, lower_ref, (1 - info_ref[0]) * width, out_ref)
        for copy in copies:
            copy.wait()

    out, gathered, *pieces = pl.pallas_call(
        kernel,
        out_shape=(pltpu.VMEM((total, width), BF16), pltpu.VMEM((total, depth), BF16), *shapes),
        in_specs=[SMEM] + [VMEM] * (len(slots) + 2) + [HBM],
        out_specs=(VMEM,) * (2 + len(spans)),
        scratch_shapes=scratch,
        cost_estimate=cost(2 * total * depth * width, 2 * depth * width),
        compiler_params=params(LIMITS[0]),
    )(info, *slots, upper, lower, later)
    return out, gathered, pieces


def up_own(info, tokens, upper, lower, later, spans):
    total, depth = tokens.shape
    width = upper.shape[1] // 2
    shapes, scratch, start = passengers(later, spans)

    def kernel(info_ref, tokens_ref, upper_ref, lower_ref, later_ref, out_ref, *rest):
        copies = start(info_ref[0], later_ref, rest[: len(spans)], rest[len(spans) :])
        product_tiles(tokens_ref, upper_ref, lower_ref, info_ref[0] * width, out_ref)
        for copy in copies:
            copy.wait()

    out, *pieces = pl.pallas_call(
        kernel,
        out_shape=(pltpu.VMEM((total, width), F32), *shapes),
        in_specs=[SMEM] + [VMEM] * 3 + [HBM],
        out_specs=(VMEM,) * (1 + len(spans)),
        scratch_shapes=scratch,
        cost_estimate=cost(2 * total * depth * width, 2 * depth * width),
        compiler_params=params(LIMITS[1]),
    )(info, tokens, upper, lower, later)
    return out, pieces


def gelu(value):
    return 0.5 * value * (1.0 + lax.erf(value * 0.7071067811865476))


def conv(info, own, received, up_bias, conv_weight, conv_bias, later, spans, groups, links, rows, grid_y):
    width = own[0].shape[1]
    slots = [(group, index) + slot for group, members in enumerate(groups) for index, slot in enumerate(members)]
    blocks = len(slots)
    total = rows * blocks
    count = len(groups)
    lanes = 128
    extent_x = total // grid_y

    shapes, scratch, start_copies = passengers(later, spans)

    def kernel(info_ref, *refs):
        own_refs, received_refs = refs[:count], refs[count : 2 * count]
        up_bias_ref, weight_ref, bias_ref, later_ref, out_ref = refs[2 * count : 2 * count + 5]
        rest = refs[2 * count + 5 :]
        hidden = rest[len(spans)]
        copies = start_copies(info_ref[0], later_ref, rest[: len(spans)], rest[len(spans) + 1 :])
        hidden[0:grid_y, :] = jnp.zeros((grid_y, lanes), F32)
        hidden[(extent_x + 1) * grid_y : (extent_x + 2) * grid_y, :] = jnp.zeros((grid_y, lanes), F32)
        at_y = lax.broadcasted_iota(jnp.int32, (grid_y, lanes), 0)
        first, last = at_y == 0, at_y == grid_y - 1
        base = info_ref[0] * width
        places = [
            links.swapped(lax.rem(info_ref[1] + (links.ring - j), links.ring)) * links.lanes
            + lax.rem(info_ref[2] + q, links.lanes)
            for _, _, q, j in slots
        ]

        def body(col, carry):
            across = pl.ds(pl.multiple_of(col * lanes, lanes), lanes)
            absolute = pl.ds(pl.multiple_of(base + col * lanes, lanes), lanes)
            shift = up_bias_ref[:, absolute]
            for slot in range(blocks):
                group, index, _, _ = slots[slot]
                down = slice(index * rows, (index + 1) * rows)
                value = own_refs[group][down, across] + received_refs[group][down, across].astype(F32) + shift
                target = pl.multiple_of(places[slot] * rows + grid_y, grid_y)
                hidden[pl.ds(target, rows), :] = value.astype(BF16).astype(F32)
            weights = [[weight_ref[a, b : b + 1, absolute] for b in range(3)] for a in range(3)]
            offset = bias_ref[:, absolute]
            for slot in range(blocks):
                for line in range(rows // grid_y):
                    start = places[slot] * rows + line * grid_y
                    near = [hidden[pl.ds(pl.multiple_of(start + a * grid_y, grid_y), grid_y), :] for a in range(3)]
                    sums = [near[0] * weights[0][b] + near[1] * weights[1][b] + near[2] * weights[2][b] for b in range(3)]
                    before = jnp.where(first, 0.0, pltpu.roll(sums[0], 1, axis=0))
                    after = jnp.where(last, 0.0, pltpu.roll(sums[2], grid_y - 1, axis=0))
                    value = sums[1] + before + after + offset
                    out_ref[slot * rows + line * grid_y : slot * rows + (line + 1) * grid_y, across] = gelu(value).astype(BF16)
            return carry

        lax.fori_loop(0, width // lanes, body, 0)
        for copy in copies:
            copy.wait()

    mixed, *pieces = pl.pallas_call(
        kernel,
        out_shape=(pltpu.VMEM((total, width), BF16), *shapes),
        in_specs=[SMEM] + [VMEM] * (2 * count + 3) + [HBM],
        out_specs=(VMEM,) * (1 + len(spans)),
        scratch_shapes=[pltpu.VMEM(((extent_x + 2) * grid_y, lanes), F32), *scratch],
        cost_estimate=cost(60 * total * width, 8 * total * width),
        compiler_params=params(LIMITS[2]),
    )(info, *own, *received, up_bias, conv_weight, conv_bias, later)
    return mixed, pieces


def dot_pieces(left_ref, down, piece_refs, across):
    right = jnp.concatenate([ref[:, across] for ref in piece_refs], axis=0)
    return jnp.dot(left_ref[down, :], right, preferred_element_type=F32)


def down_own(info, mixed, mine, later, spans):
    total, depth = mixed.shape
    width = later.shape[1]
    shapes, scratch, start = passengers(later, spans)

    def kernel(info_ref, mixed_ref, *refs):
        later_ref, out_ref = refs[len(mine) : len(mine) + 2]
        rest = refs[len(mine) + 2 :]
        copies = start(info_ref[0], later_ref, rest[: len(spans)], rest[len(spans) :])

        def body(down, col, tile):
            out_ref[down, pl.ds(col, tile)] = dot_pieces(mixed_ref, down, refs[: len(mine)], pl.ds(col, tile))

        tiles(total, width, 1024, body)
        for copy in copies:
            copy.wait()

    out, *pieces = pl.pallas_call(
        kernel,
        out_shape=(pltpu.VMEM((total, width), F32), *shapes),
        in_specs=[SMEM] + [VMEM] * (1 + len(mine)) + [HBM],
        out_specs=(VMEM,) * (1 + len(spans)),
        scratch_shapes=scratch,
        cost_estimate=cost(2 * total * depth * width, 2 * depth * width),
        compiler_params=params(LIMITS[3]),
    )(info, mixed, *mine, later)
    return out, pieces


def down_other(mixed, theirs, partial, first, outs):
    depth = mixed.shape[1]
    width = partial.shape[1]
    total = sum(rows for rows, _ in outs)
    tile = tile_of(width, 3072)

    runs, start = [], 0
    for index, (rows, _) in enumerate(outs):
        if not runs or runs[-1][1] + rows > 256:
            runs.append([start, 0, []])
        runs[-1][2].append((index, runs[-1][1], rows))
        runs[-1][1] += rows
        start += rows

    def kernel(mixed_ref, *refs):
        partial_ref, out_refs = refs[len(theirs)], refs[len(theirs) + 1 :]

        def body(step, carry):
            across = pl.ds(pl.multiple_of(step * tile, tile), tile)
            for low, high, members in runs:
                down = slice(first + low, first + low + high)
                value = partial_ref[down, across] + dot_pieces(mixed_ref, down, refs[: len(theirs)], across)
                for index, at, rows in members:
                    out_ref = out_refs[index]
                    out_ref[:, across] = value[at : at + rows].astype(out_ref.dtype)
            return carry

        lax.fori_loop(0, width // tile, body, 0)

    return pl.pallas_call(
        kernel,
        out_shape=tuple(pltpu.VMEM((rows, width), kind) for rows, kind in outs),
        in_specs=[VMEM] * (2 + len(theirs)),
        out_specs=(VMEM,) * len(outs),
        cost_estimate=cost(2 * total * depth * width, 2 * depth * width),
        compiler_params=params(10),
    )(mixed, *theirs, partial)


def finish(info, totals, bias, cols, grid_half):
    width = totals[0].shape[1]
    half = width * len(totals)

    def kernel(info_ref, *refs):
        bias_ref, stay_ref, leave_ref = refs[len(totals) :]
        core = info_ref[0]
        for index in range(len(totals)):
            shift = bias_ref[:, pl.ds(pl.multiple_of(core * half + index * width, 128), width)]
            for col in range(cols):
                for out_ref, side in ((stay_ref, core), (leave_ref, 1 - core)):
                    source = pl.ds(pl.multiple_of((2 * col + side) * grid_half, 8), grid_half)
                    out_ref[col, :, index * width : (index + 1) * width] = (refs[index][source, :] + shift).astype(BF16)

    return pl.pallas_call(
        kernel,
        out_shape=(pltpu.VMEM((cols, grid_half, half), BF16),) * 2,
        in_specs=[SMEM] + [VMEM] * (len(totals) + 1),
        out_specs=(VMEM, VMEM),
        cost_estimate=cost(4 * cols * grid_half * half, 8 * cols * grid_half * half),
        compiler_params=params(4),
    )(info, *totals, bias)


def tie(*values):
    return lax.optimization_barrier(values)


class Links:
    def __init__(self, count):
        self.lanes = 2 if count % 2 == 0 else 1
        self.ring = count // self.lanes
        self.half = self.ring // 2
        self.upward = []
        for t in range(count):
            onward = self.swapped((self.swapped(t // self.lanes) + 1) % self.ring)
            self.upward.append((t, onward * self.lanes + t % self.lanes))
        self.downward = [(t, s) for s, t in self.upward]
        self.pairs = [(t, t ^ 1) for t in range(count)]

    def swapped(self, place):
        return place ^ (place >> 1) if self.ring == 4 else place

    def up(self, value):
        return lax.ppermute(value, "tp", self.upward)

    def down(self, value):
        return lax.ppermute(value, "tp", self.downward)

    def cross(self, value):
        return lax.ppermute(value, "tp", self.pairs)


def gather(links, block, fetch_upper):
    column, beside = [block], []
    if links.lanes > 1:
        beside.append(links.cross(block))
    if links.half:
        column.append(links.up(block))
    upper = fetch_upper()
    start = block
    if links.lanes > 1:
        if links.half:
            upper, beside[0], column[1] = tie(upper, beside[0], column[1])
        if links.half + 1 < links.ring:
            start = join([block, beside[0]])
    for slot in range(1, links.half + 1):
        if slot > 1:
            column.append(links.up(column[slot - 1]))
        if links.lanes > 1:
            beside.append(links.cross(column[slot]))
    if links.half > 1 and links.half + 1 < links.ring:
        start, column[-1] = tie(start, column[-1])
    both = []
    for _ in range(links.half + 1, links.ring):
        start = links.down(start)
        both.append(start)
    early = column + beside[: links.half]
    late = beside[links.half :] + both
    names_early = [(0, j) for j in range(links.half + 1)] + [(1, j) for j in range(len(beside[: links.half]))]
    names_late = [(1, links.half)] * len(beside[links.half :])
    names_late += [(q, j) for j in range(links.ring - 1, links.half, -1) for q in range(links.lanes)]
    return early, late, [names_early] + ([names_late] if late else []), upper


def scatter(links, rows, names, late, early):
    ring, half = links.ring, links.half
    terms = {}

    def bring(make, members):
        terms.update(zip(members, make([(rows, BF16 if q else F32) for q, _ in members])))

    up_slots, down_slots = list(range(half + 1, ring)), list(range(half, 0, -1))
    order = [slot for both in zip(down_slots, up_slots) for slot in both]
    order += [slot for slot in down_slots + up_slots if slot not in order] + [0]
    crossed, arrived, ready = {}, {slot: [] for slot in range(ring)}, {}
    if len(names) > 1:
        bring(late, names[1])
    if links.lanes > 1 and half:
        crossed[half] = links.cross(terms[1, half])
    bring(early, names[0])
    if links.lanes > 1 and not half:
        crossed[0] = links.cross(terms[1, 0])
    for position, slot in enumerate(order):
        if links.lanes > 1 and position + 1 < ring:
            after = order[position + 1]
            if position == 0:
                terms[1, after], terms[0, 0] = tie(terms[1, after], terms[0, 0])
            else:
                before = order[position - 1]
                terms[1, after], ready[before] = tie(terms[1, after], ready[before])
            crossed[after] = links.cross(terms[1, after])
        total = terms[0, slot]
        for term in arrived[slot] + ([crossed[slot]] if links.lanes > 1 else []):
            total = total + term.astype(F32)
        if slot:
            ready[slot] = total.astype(BF16)
            if slot <= half:
                arrived[slot - 1].append(links.down(ready[slot]))
            else:
                arrived[(slot + 1) % ring].append(links.up(ready[slot]))
    return total


def local(tokens, up_weight, up_bias, conv_weight, conv_bias, down_weight, down_bias):
    cols, grid_half, width_model = tokens.shape
    half = width_model // 2
    part = half // 2
    units = up_weight.shape[1]
    units_half = units // 2
    grid_y = grid_half * 2
    rows = cols * grid_y

    links = Links(lax.axis_size("tp"))
    core = lax.axis_index("sp")
    mine = lax.axis_index("tp")
    swap = [(0, 1), (1, 0)]
    info = jnp.stack([core, links.swapped(mine // links.lanes), mine % links.lanes]).astype(jnp.int32)

    flat = tokens.reshape(cols * grid_half, width_model)
    whole = lax.ppermute(flat, "sp", swap)
    keep = lax.dynamic_slice_in_dim(flat, core * half, half, axis=1)
    take = lax.dynamic_slice_in_dim(whole, core * half, half, axis=1)
    keep, take = (x.reshape(cols, 1, grid_half, half) for x in (keep, take))
    block = jnp.where(core == 0, jnp.concatenate([keep, take], 1), jnp.concatenate([take, keep], 1))
    block = block.reshape(rows, half)
    block, info = tie(block, info)

    early, late, groups, upper = gather(links, block, lambda: fetch(info, up_weight, lambda c: 0 * c, part, 0))

    early_other, early_own, lower = up_early(info, early, upper, up_weight)
    third = units_half // 3 // 32 * 32
    rest = units_half - 2 * third
    late_other, late_tokens, mine_a = up_other(info, late, upper, lower, down_weight, [(0, 0, third)])
    late_own, mine_b = up_own(info, late_tokens, upper, lower, down_weight, [(0, third, third)])
    own = [early_own, late_own]
    received = [lax.ppermute(early_other, "sp", swap), lax.ppermute(late_other, "sp", swap)]
    mixed, (mine_c, theirs_a) = conv(
        info,
        own,
        received,
        up_bias.reshape(1, units),
        conv_weight,
        conv_bias.reshape(1, units),
        down_weight,
        [(0, 2 * third, rest), (1, 0, third)],
        groups,
        links,
        rows,
        grid_y,
    )
    mixed_received = lax.ppermute(mixed, "sp", swap)
    product, theirs_b = down_own(
        info, mixed, [*mine_a, *mine_b, mine_c], down_weight, [(1, third, units_half - third)]
    )
    theirs = [theirs_a, *theirs_b]

    early_rows = rows * len(groups[0])
    total = scatter(
        links,
        rows,
        groups,
        lambda outs: down_other(mixed_received, theirs, product, early_rows, outs),
        lambda outs: down_other(mixed_received, theirs, product, 0, outs),
    )

    stay, leave = finish(info, [total], down_bias.reshape(1, width_model), cols, grid_half)
    arrive = lax.ppermute(leave, "sp", swap)
    return jnp.where(core == 0, jnp.concatenate([stay, arrive], -1), jnp.concatenate([arrive, stay], -1))


def solution(mesh):
    placed = (
        P(("img", "tp"), "sp", None),
        P("sp", "tp"),
        P("tp"),
        P(None, None, "tp"),
        P("tp"),
        P("tp", "sp"),
        P(),
    )
    return jax.shard_map(
        local, mesh=mesh, in_specs=placed, out_specs=P(("img", "tp"), "sp", None), check_vma=False
    )
```

```python
import jax
import jax.numpy as jnp
from jax import lax
from jax.experimental import pallas as pl
from jax.experimental.pallas import tpu as pltpu
from jax.sharding import PartitionSpec as P

F32 = jnp.float32
BF16 = jnp.bfloat16
VMEM = pl.BlockSpec(memory_space=pltpu.VMEM)
HBM = pl.BlockSpec(memory_space=pltpu.HBM)
SMEM = pl.BlockSpec(memory_space=pltpu.SMEM)
MIB = 1 << 20
LIMITS = (24, 20, 36, 26)


def tile_of(size, most):
    for tile in range(most, 0, -128):
        if size % tile == 0:
            return tile
    return size


def cost(flops, moved, transcendentals=0):
    return pl.CostEstimate(flops=int(flops), bytes_accessed=int(moved), transcendentals=int(transcendentals))


def params(limit):
    return pltpu.CompilerParams(vmem_limit_bytes=limit * MIB)


def row_copies(weight_ref, first, out_ref, sems):
    parts = sems.shape[0]
    step = out_ref.shape[0] // parts
    return [
        pltpu.make_async_copy(
            weight_ref.at[pl.ds(first + part * step, step)], out_ref.at[pl.ds(part * step, step)], sems.at[part]
        )
        for part in range(parts)
    ]


def passengers(later, spans):
    shapes = [pltpu.VMEM((count, later.shape[1]), later.dtype) for _, _, count in spans]
    scratch = [pltpu.SemaphoreType.DMA((2,)) for _ in spans]
    units = later.shape[0] // 2

    def start(core, later_ref, out_refs, sem_refs):
        copies = []
        for (whose, first, _), out_ref, sems in zip(spans, out_refs, sem_refs):
            side = core if whose == 0 else 1 - core
            copies += row_copies(later_ref, pl.multiple_of(side * units + first, 16), out_ref, sems)
        for copy in copies:
            copy.start()
        return copies

    return shapes, scratch, start


def fetch(info, weight, start, count, held, parts=4):
    own_bytes = count * weight.shape[1] * 2
    limit = max(1, (60 * MIB - held - own_bytes) // MIB - 8)

    def kernel(info_ref, weight_ref, out_ref, sems):
        copies = row_copies(weight_ref, pl.multiple_of(start(info_ref[0]), 16), out_ref, sems)
        for copy in copies:
            copy.start()
        for copy in copies:
            copy.wait()

    return pl.pallas_call(
        kernel,
        out_shape=pltpu.VMEM((count, weight.shape[1]), weight.dtype),
        in_specs=[SMEM, HBM],
        out_specs=VMEM,
        scratch_shapes=[pltpu.SemaphoreType.DMA((parts,))],
        cost_estimate=cost(0, 2 * count * weight.shape[1] * 2),
        compiler_params=params(limit),
    )(info, weight)


def gathered_rows(slot_refs, tokens_ref):
    start = 0
    for ref in slot_refs:
        tokens_ref[start : start + ref.shape[0], :] = ref[...]
        start += ref.shape[0]


def tiles(total, width, most, body):
    tile = tile_of(width, most)
    high = tile_of(total, 256) if total > 256 else total

    def step_body(step, carry):
        row, col = step // (width // tile), step % (width // tile)
        body(pl.ds(pl.multiple_of(row * high, high), high), pl.multiple_of(col * tile, tile), tile)
        return carry

    lax.fori_loop(0, (total // high) * (width // tile), step_body, 0)


def up_early(info, slots, upper, weight):
    depth = slots[0].shape[1]
    total = sum(slot.shape[0] for slot in slots)
    split, units = upper.shape
    width = units // 2
    parts = 2
    step = (depth - split) // parts

    def kernel(info_ref, *refs):
        upper_ref, weight_ref, other_ref, own_ref, lower_ref, tokens_ref, sums_ref, sems = refs[len(slots) :]
        copies = row_copies(weight_ref, split, lower_ref, sems)
        for copy in copies:
            copy.start()
        gathered_rows(refs[: len(slots)], tokens_ref)

        def first(down, col, tile):
            across = pl.ds(col, tile)
            sums_ref[down, across] = jnp.dot(tokens_ref[down, :split], upper_ref[:, across], preferred_element_type=F32)

        tiles(total, units, 768, first)
        for part, copy in enumerate(copies):
            copy.wait()
            deep = slice(part * step, (part + 1) * step)
            features = slice(split + part * step, split + (part + 1) * step)

            def more(down, col, tile):
                across = pl.ds(col, tile)
                sums_ref[down, across] += jnp.dot(
                    tokens_ref[down, features], lower_ref[deep, across], preferred_element_type=F32
                )

            def last(out_ref, base):
                def body(down, col, tile):
                    across = pl.ds(pl.multiple_of(base + col, 128), tile)
                    value = sums_ref[down, across] + jnp.dot(
                        tokens_ref[down, features], lower_ref[deep, across], preferred_element_type=F32
                    )
                    out_ref[down, pl.ds(col, tile)] = value.astype(out_ref.dtype)

                return body

            if part < parts - 1:
                tiles(total, units, 768, more)
            else:
                tiles(total, width, 768, last(other_ref, (1 - info_ref[0]) * width))
                tiles(total, width, 768, last(own_ref, info_ref[0] * width))

    return pl.pallas_call(
        kernel,
        out_shape=(
            pltpu.VMEM((total, width), BF16),
            pltpu.VMEM((total, width), F32),
            pltpu.VMEM((depth - split, units), BF16),
        ),
        in_specs=[SMEM] + [VMEM] * (len(slots) + 1) + [HBM],
        out_specs=(VMEM,) * 3,
        scratch_shapes=[
            pltpu.VMEM((total, depth), BF16),
            pltpu.VMEM((total, units), F32),
            pltpu.SemaphoreType.DMA((parts,)),
        ],
        cost_estimate=cost(4 * total * depth * width, 2 * depth * width),
        compiler_params=params(26),
    )(info, *slots, upper, weight)


def join(parts):
    rows = sum(part.shape[0] for part in parts)

    def kernel(*refs):
        gathered_rows(refs[:-1], refs[-1])

    return pl.pallas_call(
        kernel,
        out_shape=pltpu.VMEM((rows, parts[0].shape[1]), parts[0].dtype),
        in_specs=[VMEM] * len(parts),
        out_specs=VMEM,
        cost_estimate=cost(0, 4 * rows * parts[0].shape[1]),
        compiler_params=params(1),
    )(*parts)


def product_tiles(tokens_ref, upper_ref, lower_ref, base, out_ref):
    split = upper_ref.shape[0]

    def body(down, col, tile):
        across = pl.ds(pl.multiple_of(base + col, 128), tile)
        product = jnp.dot(tokens_ref[down, :split], upper_ref[:, across], preferred_element_type=F32) + jnp.dot(
            tokens_ref[down, split:], lower_ref[:, across], preferred_element_type=F32
        )
        out_ref[down, pl.ds(col, tile)] = product.astype(out_ref.dtype)

    tiles(*out_ref.shape, 768, body)


def up_other(info, slots, upper, lower, later, spans):
    depth = slots[0].shape[1]
    total = sum(slot.shape[0] for slot in slots)
    width = upper.shape[1] // 2
    shapes, scratch, start = passengers(later, spans)

    def kernel(info_ref, *refs):
        upper_ref, lower_ref, later_ref, out_ref, tokens_ref = refs[len(slots) : len(slots) + 5]
        rest = refs[len(slots) + 5 :]
        copies = start(info_ref[0], later_ref, rest[: len(spans)], rest[len(spans) :])
        gathered_rows(refs[: len(slots)], tokens_ref)
        product_tiles(tokens_ref, upper_ref, lower_ref, (1 - info_ref[0]) * width, out_ref)
        for copy in copies:
            copy.wait()

    out, gathered, *pieces = pl.pallas_call(
        kernel,
        out_shape=(pltpu.VMEM((total, width), BF16), pltpu.VMEM((total, depth), BF16), *shapes),
        in_specs=[SMEM] + [VMEM] * (len(slots) + 2) + [HBM],
        out_specs=(VMEM,) * (2 + len(spans)),
        scratch_shapes=scratch,
        cost_estimate=cost(2 * total * depth * width, 2 * depth * width),
        compiler_params=params(LIMITS[0]),
    )(info, *slots, upper, lower, later)
    return out, gathered, pieces


def up_own(info, tokens, upper, lower, later, spans):
    total, depth = tokens.shape
    width = upper.shape[1] // 2
    shapes, scratch, start = passengers(later, spans)

    def kernel(info_ref, tokens_ref, upper_ref, lower_ref, later_ref, out_ref, *rest):
        copies = start(info_ref[0], later_ref, rest[: len(spans)], rest[len(spans) :])
        product_tiles(tokens_ref, upper_ref, lower_ref, info_ref[0] * width, out_ref)
        for copy in copies:
            copy.wait()

    out, *pieces = pl.pallas_call(
        kernel,
        out_shape=(pltpu.VMEM((total, width), F32), *shapes),
        in_specs=[SMEM] + [VMEM] * 3 + [HBM],
        out_specs=(VMEM,) * (1 + len(spans)),
        scratch_shapes=scratch,
        cost_estimate=cost(2 * total * depth * width, 2 * depth * width),
        compiler_params=params(LIMITS[1]),
    )(info, tokens, upper, lower, later)
    return out, pieces


def gelu(value):
    return 0.5 * value * (1.0 + lax.erf(value * 0.7071067811865476))


def conv(info, own, received, up_bias, conv_weight, conv_bias, later, spans, groups, links, rows, grid_y):
    width = own[0].shape[1]
    slots = [(group, index) + slot for group, members in enumerate(groups) for index, slot in enumerate(members)]
    blocks = len(slots)
    total = rows * blocks
    count = len(groups)
    lanes = 128
    extent_x = total // grid_y

    shapes, scratch, start_copies = passengers(later, spans)

    def kernel(info_ref, *refs):
        own_refs, received_refs = refs[:count], refs[count : 2 * count]
        up_bias_ref, weight_ref, bias_ref, later_ref, out_ref = refs[2 * count : 2 * count + 5]
        rest = refs[2 * count + 5 :]
        hidden = rest[len(spans)]
        copies = start_copies(info_ref[0], later_ref, rest[: len(spans)], rest[len(spans) + 1 :])
        hidden[0:grid_y, :] = jnp.zeros((grid_y, lanes), F32)
        hidden[(extent_x + 1) * grid_y : (extent_x + 2) * grid_y, :] = jnp.zeros((grid_y, lanes), F32)
        at_y = lax.broadcasted_iota(jnp.int32, (grid_y, lanes), 0)
        first, last = at_y == 0, at_y == grid_y - 1
        base = info_ref[0] * width
        places = [
            links.swapped(lax.rem(info_ref[1] + (links.ring - j), links.ring)) * links.lanes
            + lax.rem(info_ref[2] + q, links.lanes)
            for _, _, q, j in slots
        ]

        def body(col, carry):
            across = pl.ds(pl.multiple_of(col * lanes, lanes), lanes)
            absolute = pl.ds(pl.multiple_of(base + col * lanes, lanes), lanes)
            shift = up_bias_ref[:, absolute]
            for slot in range(blocks):
                group, index, _, _ = slots[slot]
                down = slice(index * rows, (index + 1) * rows)
                value = own_refs[group][down, across] + received_refs[group][down, across].astype(F32) + shift
                target = pl.multiple_of(places[slot] * rows + grid_y, grid_y)
                hidden[pl.ds(target, rows), :] = value.astype(BF16).astype(F32)
            weights = [[weight_ref[a, b : b + 1, absolute] for b in range(3)] for a in range(3)]
            offset = bias_ref[:, absolute]
            for slot in range(blocks):
                for line in range(rows // grid_y):
                    start = places[slot] * rows + line * grid_y
                    near = [hidden[pl.ds(pl.multiple_of(start + a * grid_y, grid_y), grid_y), :] for a in range(3)]
                    sums = [near[0] * weights[0][b] + near[1] * weights[1][b] + near[2] * weights[2][b] for b in range(3)]
                    before = jnp.where(first, 0.0, pltpu.roll(sums[0], 1, axis=0))
                    after = jnp.where(last, 0.0, pltpu.roll(sums[2], grid_y - 1, axis=0))
                    value = sums[1] + before + after + offset
                    out_ref[slot * rows + line * grid_y : slot * rows + (line + 1) * grid_y, across] = gelu(value).astype(BF16)
            return carry

        lax.fori_loop(0, width // lanes, body, 0)
        for copy in copies:
            copy.wait()

    mixed, *pieces = pl.pallas_call(
        kernel,
        out_shape=(pltpu.VMEM((total, width), BF16), *shapes),
        in_specs=[SMEM] + [VMEM] * (2 * count + 3) + [HBM],
        out_specs=(VMEM,) * (1 + len(spans)),
        scratch_shapes=[pltpu.VMEM(((extent_x + 2) * grid_y, lanes), F32), *scratch],
        cost_estimate=cost(60 * total * width, 8 * total * width),
        compiler_params=params(LIMITS[2]),
    )(info, *own, *received, up_bias, conv_weight, conv_bias, later)
    return mixed, pieces


def dot_pieces(left_ref, down, piece_refs, across):
    right = jnp.concatenate([ref[:, across] for ref in piece_refs], axis=0)
    return jnp.dot(left_ref[down, :], right, preferred_element_type=F32)


def down_own(info, mixed, mine, later, spans):
    total, depth = mixed.shape
    width = later.shape[1]
    shapes, scratch, start = passengers(later, spans)

    def kernel(info_ref, mixed_ref, *refs):
        later_ref, out_ref = refs[len(mine) : len(mine) + 2]
        rest = refs[len(mine) + 2 :]
        copies = start(info_ref[0], later_ref, rest[: len(spans)], rest[len(spans) :])

        def body(down, col, tile):
            out_ref[down, pl.ds(col, tile)] = dot_pieces(mixed_ref, down, refs[: len(mine)], pl.ds(col, tile))

        tiles(total, width, 1024, body)
        for copy in copies:
            copy.wait()

    out, *pieces = pl.pallas_call(
        kernel,
        out_shape=(pltpu.VMEM((total, width), F32), *shapes),
        in_specs=[SMEM] + [VMEM] * (1 + len(mine)) + [HBM],
        out_specs=(VMEM,) * (1 + len(spans)),
        scratch_shapes=scratch,
        cost_estimate=cost(2 * total * depth * width, 2 * depth * width),
        compiler_params=params(LIMITS[3]),
    )(info, mixed, *mine, later)
    return out, pieces


def down_other(mixed, theirs, partial, first, outs):
    depth = mixed.shape[1]
    width = partial.shape[1]
    total = sum(rows for rows, _ in outs)
    tile = tile_of(width, 3072)

    runs, start = [], 0
    for index, (rows, _) in enumerate(outs):
        if not runs or runs[-1][1] + rows > 256:
            runs.append([start, 0, []])
        runs[-1][2].append((index, runs[-1][1], rows))
        runs[-1][1] += rows
        start += rows

    def kernel(mixed_ref, *refs):
        partial_ref, out_refs = refs[len(theirs)], refs[len(theirs) + 1 :]

        def body(step, carry):
            across = pl.ds(pl.multiple_of(step * tile, tile), tile)
            for low, high, members in runs:
                down = slice(first + low, first + low + high)
                value = partial_ref[down, across] + dot_pieces(mixed_ref, down, refs[: len(theirs)], across)
                for index, at, rows in members:
                    out_ref = out_refs[index]
                    out_ref[:, across] = value[at : at + rows].astype(out_ref.dtype)
            return carry

        lax.fori_loop(0, width // tile, body, 0)

    return pl.pallas_call(
        kernel,
        out_shape=tuple(pltpu.VMEM((rows, width), kind) for rows, kind in outs),
        in_specs=[VMEM] * (2 + len(theirs)),
        out_specs=(VMEM,) * len(outs),
        cost_estimate=cost(2 * total * depth * width, 2 * depth * width),
        compiler_params=params(10),
    )(mixed, *theirs, partial)


def finish(info, totals, bias, cols, grid_half):
    width = totals[0].shape[1]
    half = width * len(totals)

    def kernel(info_ref, *refs):
        bias_ref, stay_ref, leave_ref = refs[len(totals) :]
        core = info_ref[0]
        for index in range(len(totals)):
            shift = bias_ref[:, pl.ds(pl.multiple_of(core * half + index * width, 128), width)]
            for col in range(cols):
                for out_ref, side in ((stay_ref, core), (leave_ref, 1 - core)):
                    source = pl.ds(pl.multiple_of((2 * col + side) * grid_half, 8), grid_half)
                    out_ref[col, :, index * width : (index + 1) * width] = (refs[index][source, :] + shift).astype(BF16)

    return pl.pallas_call(
        kernel,
        out_shape=(pltpu.VMEM((cols, grid_half, half), BF16),) * 2,
        in_specs=[SMEM] + [VMEM] * (len(totals) + 1),
        out_specs=(VMEM, VMEM),
        cost_estimate=cost(4 * cols * grid_half * half, 8 * cols * grid_half * half),
        compiler_params=params(4),
    )(info, *totals, bias)


def tie(*values):
    return lax.optimization_barrier(values)


class Links:
    def __init__(self, count):
        self.lanes = 2 if count % 2 == 0 else 1
        self.ring = count // self.lanes
        self.half = self.ring // 2
        self.upward = []
        for t in range(count):
            onward = self.swapped((self.swapped(t // self.lanes) + 1) % self.ring)
            self.upward.append((t, onward * self.lanes + t % self.lanes))
        self.downward = [(t, s) for s, t in self.upward]
        self.pairs = [(t, t ^ 1) for t in range(count)]

    def swapped(self, place):
        return place ^ (place >> 1) if self.ring == 4 else place

    def up(self, value):
        return lax.ppermute(value, "tp", self.upward)

    def down(self, value):
        return lax.ppermute(value, "tp", self.downward)

    def cross(self, value):
        return lax.ppermute(value, "tp", self.pairs)


def gather(links, block, fetch_upper):
    column, beside = [block], []
    if links.lanes > 1:
        beside.append(links.cross(block))
    if links.half:
        column.append(links.up(block))
    upper = fetch_upper()
    start = block
    if links.lanes > 1:
        if links.half:
            upper, beside[0], column[1] = tie(upper, beside[0], column[1])
        if links.half + 1 < links.ring:
            start = join([block, beside[0]])
    for slot in range(1, links.half + 1):
        if slot > 1:
            column.append(links.up(column[slot - 1]))
        if links.lanes > 1:
            beside.append(links.cross(column[slot]))
    if links.half > 1 and links.half + 1 < links.ring:
        start, column[-1] = tie(start, column[-1])
    both = []
    for _ in range(links.half + 1, links.ring):
        start = links.down(start)
        both.append(start)
    early = column + beside[: links.half]
    late = beside[links.half :] + both
    names_early = [(0, j) for j in range(links.half + 1)] + [(1, j) for j in range(len(beside[: links.half]))]
    names_late = [(1, links.half)] * len(beside[links.half :])
    names_late += [(q, j) for j in range(links.ring - 1, links.half, -1) for q in range(links.lanes)]
    return early, late, [names_early] + ([names_late] if late else []), upper


def scatter(links, rows, names, late, early):
    ring, half = links.ring, links.half
    terms = {}

    def bring(make, members):
        terms.update(zip(members, make([(rows, BF16 if q else F32) for q, _ in members])))

    up_slots, down_slots = list(range(half + 1, ring)), list(range(half, 0, -1))
    order = [slot for both in zip(down_slots, up_slots) for slot in both]
    order += [slot for slot in down_slots + up_slots if slot not in order] + [0]
    crossed, arrived, ready = {}, {slot: [] for slot in range(ring)}, {}
    if len(names) > 1:
        bring(late, names[1])
    if links.lanes > 1 and half:
        crossed[half] = links.cross(terms[1, half])
    bring(early, names[0])
    if links.lanes > 1 and not half:
        crossed[0] = links.cross(terms[1, 0])
    for position, slot in enumerate(order):
        if links.lanes > 1 and position + 1 < ring:
            after = order[position + 1]
            if position == 0:
                terms[1, after], terms[0, 0] = tie(terms[1, after], terms[0, 0])
            else:
                before = order[position - 1]
                terms[1, after], ready[before] = tie(terms[1, after], ready[before])
            crossed[after] = links.cross(terms[1, after])
        total = terms[0, slot]
        for term in arrived[slot] + ([crossed[slot]] if links.lanes > 1 else []):
            total = total + term.astype(F32)
        if slot:
            ready[slot] = total.astype(BF16)
            if slot <= half:
                arrived[slot - 1].append(links.down(ready[slot]))
            else:
                arrived[(slot + 1) % ring].append(links.up(ready[slot]))
    return total


def local(tokens, up_weight, up_bias, conv_weight, conv_bias, down_weight, down_bias):
    cols, grid_half, width_model = tokens.shape
    half = width_model // 2
    part = half // 2
    units = up_weight.shape[1]
    units_half = units // 2
    grid_y = grid_half * 2
    rows = cols * grid_y

    links = Links(lax.axis_size("tp"))
    core = lax.axis_index("sp")
    mine = lax.axis_index("tp")
    swap = [(0, 1), (1, 0)]
    info = jnp.stack([core, links.swapped(mine // links.lanes), mine % links.lanes]).astype(jnp.int32)

    flat = tokens.reshape(cols * grid_half, width_model)
    whole = lax.ppermute(flat, "sp", swap)
    keep = lax.dynamic_slice_in_dim(flat, core * half, half, axis=1)
    take = lax.dynamic_slice_in_dim(whole, core * half, half, axis=1)
    keep, take = (x.reshape(cols, 1, grid_half, half) for x in (keep, take))
    block = jnp.where(core == 0, jnp.concatenate([keep, take], 1), jnp.concatenate([take, keep], 1))
    block = block.reshape(rows, half)
    block, info = tie(block, info)

    early, late, groups, upper = gather(links, block, lambda: fetch(info, up_weight, lambda c: 0 * c, part, 0))

    early_other, early_own, lower = up_early(info, early, upper, up_weight)
    third = units_half // 3 // 32 * 32
    rest = units_half - 2 * third
    less = third * 3 // 4 // 32 * 32
    late_other, late_tokens, mine_a = up_other(info, late, upper, lower, down_weight, [(0, 0, third)])
    late_own, mine_b = up_own(info, late_tokens, upper, lower, down_weight, [(0, third, third)])
    own = [early_own, late_own]
    received = [lax.ppermute(early_other, "sp", swap), lax.ppermute(late_other, "sp", swap)]
    mixed, (mine_c, theirs_a) = conv(
        info,
        own,
        received,
        up_bias.reshape(1, units),
        conv_weight,
        conv_bias.reshape(1, units),
        down_weight,
        [(0, 2 * third, rest), (1, 0, less)],
        groups,
        links,
        rows,
        grid_y,
    )
    mixed_received = lax.ppermute(mixed, "sp", swap)
    product, theirs_b = down_own(
        info, mixed, [*mine_a, *mine_b, mine_c], down_weight, [(1, less, units_half - less)]
    )
    theirs = [theirs_a, *theirs_b]

    early_rows = rows * len(groups[0])
    total = scatter(
        links,
        rows,
        groups,
        lambda outs: down_other(mixed_received, theirs, product, early_rows, outs),
        lambda outs: down_other(mixed_received, theirs, product, 0, outs),
    )

    stay, leave = finish(info, [total], down_bias.reshape(1, width_model), cols, grid_half)
    arrive = lax.ppermute(leave, "sp", swap)
    return jnp.where(core == 0, jnp.concatenate([stay, arrive], -1), jnp.concatenate([arrive, stay], -1))


def solution(mesh):
    placed = (
        P(("img", "tp"), "sp", None),
        P("sp", "tp"),
        P("tp"),
        P(None, None, "tp"),
        P("tp"),
        P("tp", "sp"),
        P(),
    )
    return jax.shard_map(
        local, mesh=mesh, in_specs=placed, out_specs=P(("img", "tp"), "sp", None), check_vma=False
    )
```
